32 devices in a mesh: hot: 4 (over y, x), tt: 8 (over z, core).
Axes of the slice: x: 2, y: 2, z: 4, core: 2. Of those that a mesh axis runs over, the one named last changes fastest.
Arguments:
- hot_table: float32 [1024, 256], P('hot'), may hold values from -1.5 to 1.5
- hot_accum: float32 [1024], P('hot'), may hold values from 0.05 to 1
- hot_owner: int32 [8192, 1], P(('hot', 'tt')), may hold values from 0 to 3; in each aligned block of 256 rows (0 to 255, 256 to 511, ...) at most 128 rows name the same one
- hot_row: int32 [32, 256], P(('hot', 'tt')), may hold values from 0 to 255
- hot_bag: int32 [32, 256], P(('hot', 'tt')), may hold values from 0 to 63, never falling along the last dimension, each value on 1 to 12 neighbouring positions
- cold_owner: int32 [16384, 1], P(('hot', 'tt')), may hold values from 0 to 7; in each aligned block of 512 rows (0 to 511, 512 to 1023, ...) at most 128 rows name the same one
- first_index: int32 [32, 512], P(('hot', 'tt')), may hold values from 0 to 127
- mid_index: int32 [32, 512], P(('hot', 'tt')), may hold values from 0 to 63
- last_index: int32 [32, 512], P(('hot', 'tt')), may hold values from 0 to 63
- cold_bag: int32 [32, 512], P(('hot', 'tt')), may hold values from 0 to 63, never falling along the last dimension, each value on 1 to 24 neighbouring positions
- core_first: float32 [1024, 256], P('tt'), may hold values from -1 to 1
- core_mid: bfloat16 [64, 8192], replicated, may hold values from -1 to 1
- core_last: bfloat16 [64, 128], replicated, may hold values from -6 to 6
- bag_grads: bfloat16 [2048, 256], P(('hot', 'tt')), may hold values from -6 to 6
Outputs:
- pooled: float32 [2048, 256], P(('hot', 'tt'))
- new_table: float32 [1024, 256], P('hot')
- new_accum: float32 [1024], P('hot')
- new_first: float32 [1024, 256], P('tt')
The draws below stay inside these ranges and needn't reach their ends.
Inputs may be any that keep to these rules, and one draw needn't show every extreme that they name: `hot_owner`: among the 256 hot lookups of one device no owner appears more than 128 times; some owner appears exactly that often. `cold_owner`: among the 512 cold lookups of one device no owner appears more than 128 times; some owner appears exactly that often. `hot_bag`: never falling along a device's lookups; every bag of a device has at least one hot lookup. `cold_bag`: never falling along a device's lookups; every bag of a device has at least one cold lookup.
All inputs are finite; a program needn't handle non-finite values.
Results may differ from the reference program's by a relative error of at most 0.005.
Values may be sent and summed in bfloat16 or wider, within the bound.
No kernel may reach another device: no remote copies, remote signals or barrier semaphores. Data moves between devices by JAX's collectives and lax.ppermute only.
A program may use at most 64 MiB of HBM per device.

```python
import math
import jax
import jax.numpy as jnp
import numpy as np
from jax import lax

E1 = 8
E2 = 8
E3 = 4
RANK = 32
HOT_DEV = 256
HOT_LOOK = 256
COLD_LOOK = 512
BAGS_DEV = 64
SLICE_DEV = 128
MID_SLICES = 64
LAST_SLICES = 64
E = 256
CAP_HOT = 128
CAP_COLD = 128
N_HOT = 4
N_TT = 8
DEVICES = 32


def touch_ends(values, key, least, top_value):
    place = [jax.random.randint(jax.random.fold_in(key, axis), (), 0, length) for axis, length in enumerate(values.shape)]
    main_axis = values.shape.index(max(values.shape))
    beside = place[:main_axis] + [(place[main_axis] + 1) % values.shape[main_axis]] + place[main_axis + 1:]
    return values.at[tuple(place)].set(least).at[tuple(beside)].set(top_value)


def levels(key, extent, cuts, low, high):
    def one(axis_at, shards_of):
        draws = jax.random.uniform(jax.random.fold_in(jax.random.fold_in(key, 6), axis_at), (shards_of,), jnp.float32, low / len(cuts), high / len(cuts))
        return jnp.repeat(jnp.exp(draws), extent[axis_at] // shards_of).reshape((-1,) + (1,) * (len(extent) - axis_at - 1))

    level = one(*cuts[0])
    for cut in cuts[1:]:
        level = level * one(*cut)
    return level


def rank_bounds(count, slope):
    portions = [(1 << 20) // math.isqrt(rank ** slope) + 1 for rank in range(1, count + 1)]
    deviation = 1 + sum(portions) // (1 << 30)
    return np.cumsum(np.array([max(1, weight // deviation) for weight in portions]))


def ranked_ids(stream_key, shape, amount, skew):
    grid = rank_bounds(amount, skew)
    pick = jax.random.randint(jax.random.fold_in(stream_key, 1), shape, 0, int(grid[amount - 1]))
    grade = jnp.searchsorted(jnp.asarray(grid, jnp.int32), pick, side="right")
    return jax.random.permutation(jax.random.fold_in(stream_key, 2), amount)[grade].astype(jnp.int32)


def split_up(count, total, limit, lean):
    portions = [(1 << 20) // math.isqrt(rank ** lean) + 1 for rank in range(2, count + 1)]
    surplus, given = total - limit - (count - 1), [1] * (count - 1)
    while surplus > 0:
        candidates = [i for i in range(count - 1) if given[i] < limit]
        whole, left = sum([portions[i] for i in candidates]), surplus
        for i in candidates:
            more = min(limit - given[i], max(1, left * portions[i] // whole), surplus)
            given[i] = given[i] + more
            surplus = surplus - more
    return np.array([limit] + given)


def ragged_sizes(rng, number_of, total, bound, slope):
    if number_of == 2:
        one = jax.random.randint(rng, (), max(1, total - bound), min(bound, total - 1) + 1)
        return jnp.stack([one, total - one])
    sizes = jnp.asarray(split_up(number_of, total, bound, slope), jnp.int32)
    twos = (number_of - 1) // 2
    source_of, taker = sizes[1:1 + 2 * twos:2], sizes[2:2 + 2 * twos:2]
    slack = jnp.minimum(source_of - 1, bound - taker)
    shifted = jax.random.randint(jax.random.fold_in(rng, 1), (twos,), 0, 1 << 20) % (slack + 1)
    sizes = sizes.at[1:1 + 2 * twos:2].set(source_of - shifted).at[2:2 + 2 * twos:2].set(taker + shifted)
    return sizes[jax.random.permutation(jax.random.fold_in(rng, 2), number_of)]


def deal_out(own_key, own, number, rows, number_of, top, most, lean):
    sequence = jax.random.permutation(own_key, number_of)
    heavy_load, common = portions_of(number_of, rows * top, most, lean, True), portions_of(number_of, rows * top, most, lean, False)
    places = jnp.arange(number_of)

    def named(tallies, rotation):
        used = int((tallies > 0).sum())
        fixed = max(1, used // 4)
        moved = fixed + (places - fixed + rotation * (used - fixed)) % max(1, number_of - fixed)
        return jnp.zeros((number_of,), jnp.int32).at[sequence[jnp.where(places < fixed, places, moved)]].set(jnp.asarray(tallies, jnp.int32))

    tallies = jnp.where(number % 4 == 0, named(heavy_load, number // 4), named(common, number - number // 4 - 1))
    mixed = jax.random.permutation(jax.random.fold_in(own, 3), number_of)
    giver, receiver = mixed[0:number_of // 2 * 2:2], mixed[1:number_of // 2 * 2:2]
    room = jnp.minimum(tallies[giver] - 1, most - tallies[receiver]) // 2
    room = jnp.where((giver == sequence[0]) | (receiver == sequence[0]) | (tallies[receiver] == 0), 0, jnp.maximum(room, 0))
    moved = jax.random.randint(jax.random.fold_in(own, 4), (number_of // 2,), 0, 1 << 20) % (room + 1)
    tallies = tallies.at[giver].add(-moved).at[receiver].add(moved)
    members = jnp.searchsorted(jnp.cumsum(tallies), jnp.arange(rows * top), side="right").astype(jnp.int32)
    table = members.reshape(top, rows).T
    table = table[jax.random.permutation(jax.random.fold_in(own, 1), rows)]
    rotation = jax.random.randint(jax.random.fold_in(own, 2), (rows, 1), 0, top)
    return jnp.take_along_axis(table, (jnp.arange(top)[None, :] + rotation) % top, axis=1)


def portions_of(number_of, total, bound, lean, full):
    loads = [(1 << 20) // math.isqrt(rank ** lean) + 1 for rank in range(1, number_of + 1)]
    largest = bound if full else min(bound, max(-(-total // number_of), total * loads[0] // sum(loads)))
    least = 1 if total - largest >= number_of - 1 else 0
    holding, rest = [largest] + [least] * (number_of - 1), total - largest - least * (number_of - 1)
    while rest > 0:
        candidates = [i for i in range(1, number_of) if holding[i] < largest] or [i for i in range(1, number_of) if holding[i] < bound]
        pool, left = sum([loads[i] for i in candidates]), rest
        for i in candidates:
            addition = min(bound - holding[i], max(1, left * loads[i] // pool), rest)
            holding[i] = holding[i] + addition
            rest = rest - addition
    return np.array(holding)


def scatter_about(rng, extent, deviation, reach, shards=(), held_as=jnp.bfloat16):
    entries = jax.random.normal(rng, extent, jnp.float32) * deviation
    if len(shards) > 0:
        entries = levels(rng, extent, shards, -0.22, 0.18) * entries
    return jnp.clip(entries, min=-reach, max=reach).astype(held_as)


def setup_inputs(seed: int = 0) -> dict:
    arg_keys = jax.random.split(jax.random.key(seed), 15)
    hot_table = scatter_about(arg_keys[0], (N_HOT * HOT_DEV, E), 0.25, 1.5, ((0, 4),), jnp.float32)
    hot_accum = jnp.clip(jnp.exp(math.log(1.0) - 2.9957323 * jax.random.uniform(arg_keys[1], (N_HOT * HOT_DEV,), jnp.float32) ** levels(arg_keys[1], (N_HOT * HOT_DEV,), ((0, 4),), -0.2, 0.2)), 0.05, 1.0)
    hot_owner_keys = jax.random.split(jax.random.fold_in(arg_keys[2], 1), (DEVICES * HOT_LOOK) // HOT_LOOK)
    hot_owner_turns = jax.random.permutation(jax.random.fold_in(arg_keys[2], 3), (DEVICES * HOT_LOOK) // HOT_LOOK)
    hot_owner = jax.vmap(lambda own, number: deal_out(jax.random.fold_in(arg_keys[2], 2), own, number, HOT_LOOK, N_HOT, 1, CAP_HOT, 2))(hot_owner_keys, hot_owner_turns).reshape((DEVICES * HOT_LOOK, 1))
    hot_row = touch_ends(ranked_ids(arg_keys[3], (DEVICES, HOT_LOOK), HOT_DEV, 2), jax.random.fold_in(arg_keys[3], 3), 0, HOT_DEV - 1).astype(jnp.int32)
    hot_bag = jax.vmap(lambda own: jnp.searchsorted(jnp.cumsum(ragged_sizes(own, BAGS_DEV, HOT_LOOK, 3 * HOT_LOOK // BAGS_DEV, 2)), jnp.arange(HOT_LOOK), side="right"))(jax.random.split(arg_keys[4], DEVICES)).reshape((DEVICES, HOT_LOOK)).astype(jnp.int32)
    cold_owner_keys = jax.random.split(jax.random.fold_in(arg_keys[5], 1), (DEVICES * COLD_LOOK) // COLD_LOOK)
    cold_owner_turns = jax.random.permutation(jax.random.fold_in(arg_keys[5], 3), (DEVICES * COLD_LOOK) // COLD_LOOK)
    cold_owner = jax.vmap(lambda own, number: deal_out(jax.random.fold_in(arg_keys[5], 2), own, number, COLD_LOOK, N_TT, 1, CAP_COLD, 2))(cold_owner_keys, cold_owner_turns).reshape((DEVICES * COLD_LOOK, 1))
    first_index = touch_ends(jax.random.randint(arg_keys[6], (DEVICES, COLD_LOOK), 0, SLICE_DEV), jax.random.fold_in(arg_keys[6], 1), 0, SLICE_DEV - 1).astype(jnp.int32)
    mid_index = touch_ends(ranked_ids(arg_keys[7], (DEVICES, COLD_LOOK), MID_SLICES, 1), jax.random.fold_in(arg_keys[7], 3), 0, MID_SLICES - 1).astype(jnp.int32)
    last_index = touch_ends(jax.random.randint(arg_keys[8], (DEVICES, COLD_LOOK), 0, LAST_SLICES), jax.random.fold_in(arg_keys[8], 1), 0, LAST_SLICES - 1).astype(jnp.int32)
    cold_bag = jax.vmap(lambda own: jnp.searchsorted(jnp.cumsum(ragged_sizes(own, BAGS_DEV, COLD_LOOK, 3 * COLD_LOOK // BAGS_DEV, 2)), jnp.arange(COLD_LOOK), side="right"))(jax.random.split(arg_keys[9], DEVICES)).reshape((DEVICES, COLD_LOOK)).astype(jnp.int32)
    core_first = scatter_about(arg_keys[10], (N_TT * SLICE_DEV, E1 * RANK), RANK ** -0.5, 1.0, ((0, 8),), jnp.float32)
    core_mid = scatter_about(arg_keys[11], (MID_SLICES, RANK * E2 * RANK), RANK ** -0.5, 1.0)
    core_last = scatter_about(arg_keys[12], (LAST_SLICES, RANK * E3), 1.0, 6.0)
    bag_grads = scatter_about(arg_keys[13], (DEVICES * BAGS_DEV, E), 1.0, 6.0, ((0, 32),))
    return dict(hot_table=hot_table, hot_accum=hot_accum, hot_owner=hot_owner, hot_row=hot_row, hot_bag=hot_bag, cold_owner=cold_owner, first_index=first_index, mid_index=mid_index, last_index=last_index, cold_bag=cold_bag, core_first=core_first, core_mid=core_mid, core_last=core_last, bag_grads=bag_grads)


def rounded(values):
    return lax.optimization_barrier(values.astype(jnp.bfloat16)).astype(jnp.float32)

def reference(hot_table, hot_accum, hot_owner, hot_row, hot_bag, cold_owner, first_index, mid_index, last_index, cold_bag, core_first, core_mid, core_last, bag_grads):
    devices_all = hot_bag.shape[0]
    bag_count = BAGS_DEV
    feature_width = E1 * E2 * E3
    tail_width = E2 * E3
    hot_keys = hot_owner[:, 0].reshape(devices_all, -1) * HOT_DEV + hot_row
    fetched = rounded(hot_table[hot_keys.reshape(-1)])
    device_ids = jnp.arange(devices_all, dtype=jnp.int32)[:, None]
    hot_global = (device_ids * bag_count + hot_bag).reshape(-1).astype(jnp.int32)
    pooled_hot = jax.ops.segment_sum(fetched, hot_global, devices_all * bag_count)
    hot_cot = bag_grads[hot_global].astype(jnp.float32)
    row_grad = jax.ops.segment_sum(hot_cot, hot_keys.reshape(-1), N_HOT * HOT_DEV)
    new_accum = hot_accum + lax.optimization_barrier(jnp.mean(row_grad * row_grad, axis=1))
    new_table = hot_table - 0.1 * row_grad / (jnp.sqrt(new_accum)[:, None] + 1e-08)
    first_global = cold_owner[:, 0].reshape(devices_all, -1) * SLICE_DEV + first_index
    grads_by_device = bag_grads.reshape(devices_all, bag_count, feature_width)

    def one_device(inputs):
        first_rows, middle, lasts, bags, grads = inputs
        mid_cores = core_mid[middle].astype(jnp.float32).reshape(-1, RANK, E2, RANK)
        last_cores = core_last[lasts].astype(jnp.float32).reshape(-1, RANK, E3)
        maps = rounded(jnp.einsum('nawb,nbe->nawe', mid_cores, last_cores).reshape(-1, RANK, tail_width))
        slices = rounded(core_first[first_rows]).reshape(-1, E1, RANK)
        cold_rows = rounded(jnp.einsum('kea,kaj->kej', slices, maps).reshape(-1, feature_width))
        pooled_cold = jax.ops.segment_sum(cold_rows, bags, bag_count)
        cotangent = grads[bags].astype(jnp.float32).reshape(-1, E1, tail_width)
        terms = jnp.einsum('kej,kaj->kea', cotangent, maps).reshape(-1, E1 * RANK)
        return (pooled_cold, terms)
    pooled_cold, terms = lax.map(one_device, (first_global, mid_index, last_index, cold_bag, grads_by_device))
    core_grad = jax.ops.segment_sum(terms.reshape(-1, E1 * RANK), first_global.reshape(-1), N_TT * SLICE_DEV)
    new_first = core_first - 0.01 * core_grad
    pooled = pooled_hot + pooled_cold.reshape(devices_all * bag_count, feature_width)
    return (pooled, new_table, new_accum, new_first)
```

```python
import jax
import jax.numpy as jnp
from jax import lax
from jax.experimental import pallas as pl
from jax.experimental.pallas import tpu as pltpu
from jax.sharding import PartitionSpec as P

E1 = 8
E2 = 8
E3 = 4
RANK = 32
TAIL = E2 * E3
LANES = 128
PAD = 16
F32 = jnp.float32
BF16 = jnp.bfloat16
NT = (((1,), (1,)), ((), ()))


def iota(shape, dim):
    return lax.broadcasted_iota(jnp.int32, shape, dim)


def hot(mask):
    return mask.astype(F32).astype(BF16)


def mm(a, b):
    return jnp.dot(a, b, preferred_element_type=F32)


def mm_nt(a, b):
    return lax.dot_general(a, b, NT, preferred_element_type=F32)


def call(body, name, outs, scratch=()):
    return pl.pallas_call(
        body,
        out_shape=tuple(jax.ShapeDtypeStruct(s, d) for s, d in outs),
        scratch_shapes=[pltpu.VMEM(s, d) for s, d in scratch],
        name=name,
    )


def smem():
    return pl.BlockSpec(memory_space=pltpu.SMEM)


def pack_kernel(table, grads, owner, row, bag, first, hot_out, first_out):
    rows, bags = table.shape[0], grads.shape[0]
    looks = jnp.concatenate(
        [owner[...], row[...], bag[...], jnp.zeros((PAD - 3, row.shape[1]), jnp.int32)], axis=0
    )
    turned = first[...].T.astype(BF16)
    for peer in range(hot_out.shape[0]):
        hot_out[peer, 0:rows, :] = table[...].astype(BF16)
        hot_out[peer, rows : rows + bags, :] = grads[...]
        hot_out[peer, rows + bags :, :] = looks.astype(F32).astype(BF16)
    for peer in range(first_out.shape[0]):
        first_out[peer] = turned


def maps_kernel(
    side, mid, last, mid_index, last_index, bag, owner, index, grads,
    keep, send, maps, turned, left, right, lasts_of, cot, terms,
):
    mids, lasts = mid.shape[0], last.shape[0]
    looks = bag.shape[1]

    def turn(t, _):
        at = pl.ds(pl.multiple_of(t * LANES, LANES), LANES)
        block = mid[:, at].astype(F32)
        turned[at, :] = jnp.concatenate([block, block], axis=0).T
        return 0

    lax.fori_loop(0, mid.shape[1] // LANES, turn, 0, unroll=4)
    first_half = iota((RANK * E2, 2 * mids), 1) < mids
    for pair in range(RANK // 2):
        low = turned[pl.ds(2 * pair, RANK * E2, stride=RANK), :]
        high = turned[pl.ds(2 * pair + 1, RANK * E2, stride=RANK), :]
        left[:, pair * 2 * mids : (pair + 1) * 2 * mids] = jnp.where(first_half, low, high).astype(BF16)
    pick_last = hot(iota((lasts, looks), 0) == last_index[...])
    lasts_of[...] = mm(last[...].astype(F32).T.astype(BF16), pick_last)
    pick_bag = hot(iota((grads.shape[0], looks), 0) == bag[...])
    cot[...] = mm(grads[...].astype(F32).T.astype(BF16), pick_bag)
    pick_mid = hot(iota((mids, looks), 0) == mid_index[...])
    for e3 in range(E3):
        for b in range(RANK):
            at = b * E3 + e3
            spread = jnp.broadcast_to(lasts_of[at : at + 1, :], (PAD, looks)).astype(BF16)
            for part in range(0, mids, PAD):
                right[b * mids + part : b * mids + part + PAD, :] = pick_mid[part : part + PAD, :] * spread
        made = mm(left[...], right[...]).astype(BF16).astype(F32)
        for t in range(looks // LANES):
            maps[t, e3 * RANK * E2 : (e3 + 1) * RANK * E2, :] = made[:, t * LANES : (t + 1) * LANES]

    def back(t, _):
        lanes = pl.ds(pl.multiple_of(t * LANES, LANES), LANES)
        sums = [jnp.zeros((RANK, LANES), F32) for _ in range(E1)]
        for e2 in range(E2):
            for e3 in range(E3):
                part = maps[t, pl.ds(e3 * RANK * E2 + e2, RANK, stride=E2), :]
                for e1 in range(E1):
                    at = e1 * TAIL + e2 * E3 + e3
                    sums[e1] = sums[e1] + part * cot[at : at + 1, lanes]
        for e1 in range(E1):
            terms[e1 * RANK : (e1 + 1) * RANK, lanes] = sums[e1]
        return 0

    lax.fori_loop(0, looks // LANES, back, 0)
    whole = terms[...]
    high = whole.astype(BF16)
    low = (whole - high.astype(F32)).astype(BF16)
    own = owner[...]
    held = keep.shape[0]
    slices = held // side[1]
    key = ((own & 1) ^ side[0]) * held + (own >> 1) * slices + index[...]
    step = min(held, 256)
    for half, out in ((0, keep), (1, send)):
        for start in range(0, held, step):
            pick = hot(iota((step, looks), 0) + (half * held + start) == key)
            out[start : start + step, :] = (mm_nt(pick, high) + mm_nt(pick, low)).astype(out.dtype)


def hot_kernel(side, gathered, owner, row, bag, keep, send, pooled):
    peers, bags = gathered.shape[0], pooled.shape[0]
    looks = row.shape[1]
    half = keep.shape[0]
    rows = 2 * half
    at = iota((rows, looks), 0)
    pick_bag = hot(iota((bags, looks), 0) == bag[...])
    mine = row[...]
    total = jnp.zeros(pooled.shape, F32)
    for peer in range(peers):
        pick = hot((at == mine) & (owner[...] == peer))
        total = total + mm(mm_nt(pick_bag, pick).astype(BF16), gathered[peer, 0:rows, :])
    pooled[...] = total
    grad = jnp.zeros((rows, pooled.shape[1]), F32)
    for peer in range(peers):
        sent = gathered[peer, rows + bags :, :].astype(F32).astype(jnp.int32)
        theirs, place, their_bag = sent[0:1, :], sent[1:2, :], sent[2:3, :]
        upper = (place >= half).astype(jnp.int32)
        place = (upper ^ side[0]) * half + place - upper * half
        pick = hot((at == place) & (theirs == side[1]))
        count = mm_nt(pick, hot(iota((bags, looks), 0) == their_bag))
        grad = grad + mm(count.astype(BF16), gathered[peer, rows : rows + bags, :])
    keep[...] = grad[0:half]
    send[...] = grad[half:].astype(BF16)


def pair_kernel(cold_keep, cold_got, hot_keep, hot_got, out):
    peers = out.shape[0]
    slices = cold_keep.shape[0] // peers
    hot_sum = (hot_keep[...] + hot_got[...].astype(F32)).astype(BF16)
    for peer in range(peers):
        at = slice(peer * slices, (peer + 1) * slices)
        out[peer, 0:slices, :] = (cold_keep[at, :] + cold_got[at, :].astype(F32)).astype(BF16)
        out[peer, slices:, :] = hot_sum


def line_kernel(got, cold, hot_half):
    slices = cold.shape[1]
    total = got[0].astype(F32)
    for peer in range(1, got.shape[0]):
        total = total + got[peer].astype(F32)
    sent = total[0:slices].astype(BF16)
    for peer in range(cold.shape[0]):
        cold[peer] = sent
    hot_half[...] = total[slices:]


def rows_kernel(gathered, maps, owner, index, bag, hot_part, pooled, slices_of, rows):
    peers, width, slices = gathered.shape
    looks = bag.shape[1]
    tiles = looks // LANES
    key = owner[...] * slices + index[...]
    total = jnp.zeros((width, looks), F32)
    for peer in range(peers):
        pick = hot(iota((slices, looks), 0) + peer * slices == key)
        total = total + mm(gathered[peer], pick)
    for t in range(tiles):
        slices_of[t] = total[:, t * LANES : (t + 1) * LANES]

    def forward(t, _):
        sums = [[jnp.zeros((E2, LANES), F32) for _ in range(E3)] for _ in range(E1)]
        for a in range(RANK):
            parts = [maps[t, e3 * RANK * E2 + a * E2 : e3 * RANK * E2 + a * E2 + E2, :] for e3 in range(E3)]
            for e1 in range(E1):
                entry = slices_of[t, e1 * RANK + a : e1 * RANK + a + 1, :]
                for e3 in range(E3):
                    sums[e1][e3] = sums[e1][e3] + parts[e3] * entry
        for e1 in range(E1):
            for e3 in range(E3):
                rows[t, pl.ds(e1 * TAIL + e3, E2, stride=E3), :] = sums[e1][e3]
        return 0

    lax.fori_loop(0, tiles, forward, 0)
    out = hot_part[...]
    for t in range(tiles):
        pick = hot(iota((pooled.shape[0], LANES), 0) == bag[:, t * LANES : (t + 1) * LANES])
        out = out + mm_nt(pick, rows[t].astype(BF16))
    pooled[...] = out


def final_kernel(side, cold, first, mine, other, table, accum, new_first, new_table, new_accum):
    total = cold[0].astype(F32)
    for peer in range(1, cold.shape[0]):
        total = total + cold[peer].astype(F32)
    new_first[...] = first[...] - 0.01 * total
    lower = side[0] == 0
    grad = jnp.concatenate(
        [jnp.where(lower, mine[...], other[...]), jnp.where(lower, other[...], mine[...])], axis=0
    )
    rows = grad.shape[0]
    mean = jnp.mean(grad * grad, axis=1, keepdims=True)
    held = jnp.broadcast_to(accum[...], (LANES, rows)).T + mean
    new_accum[...] = held.T[0:1, :]
    new_table[...] = table[...] - 0.1 * grad / (jnp.sqrt(held[:, 0:1]) + 1e-08)


def local(
    hot_table, hot_accum, hot_owner, hot_row, hot_bag, cold_owner, first_index,
    mid_index, last_index, cold_bag, core_first, core_mid, core_last, bag_grads,
):
    rows, width = hot_table.shape
    bags = bag_grads.shape[0]
    slices = core_first.shape[0]
    hot_peers, tt_peers = lax.axis_size("hot"), lax.axis_size("tt")
    pairs = tt_peers // 2
    looks = cold_bag.shape[1]
    assert max(rows, bags, hot_peers) <= 256
    core = lax.axis_index("tt") % 2
    owner = hot_owner.reshape(1, -1)
    slice_owner = cold_owner.reshape(1, -1)
    swap = [(i, i ^ 1) for i in range(tt_peers)]

    hot_pack, first_pack = call(
        pack_kernel, "pack",
        (((hot_peers, rows + bags + PAD, width), BF16), ((tt_peers, width, slices), BF16)),
    )(hot_table, bag_grads, owner, hot_row, hot_bag, core_first)
    hot_all = lax.all_to_all(hot_pack, "hot", 0, 0, tiled=True)
    first_all = lax.all_to_all(first_pack, "tt", 0, 0, tiled=True)

    held = slices * pairs
    side = jnp.stack([core, jnp.int32(pairs)])
    keep, send, maps = pl.pallas_call(
        maps_kernel,
        out_shape=(
            jax.ShapeDtypeStruct((held, width), F32),
            jax.ShapeDtypeStruct((held, width), BF16),
            jax.ShapeDtypeStruct((looks // LANES, E3 * RANK * E2, LANES), F32),
        ),
        in_specs=[smem()] + [pl.BlockSpec(memory_space=pltpu.VMEM)] * 8,
        scratch_shapes=[
            pltpu.VMEM((core_mid.shape[1], LANES), F32),
            pltpu.VMEM((RANK * E2, RANK * core_mid.shape[0]), BF16),
            pltpu.VMEM((RANK * core_mid.shape[0], looks), BF16),
            pltpu.VMEM((RANK * E3, looks), F32),
            pltpu.VMEM((width, looks), F32),
            pltpu.VMEM((width, looks), F32),
        ],
        name="maps",
    )(side, core_mid, core_last, mid_index, last_index, cold_bag, slice_owner, first_index, bag_grads)
    got = lax.ppermute(send, "tt", swap)

    side = jnp.stack([core, lax.axis_index("hot")])
    hot_keep, hot_send, hot_part = pl.pallas_call(
        hot_kernel,
        out_shape=(
            jax.ShapeDtypeStruct((rows // 2, width), F32),
            jax.ShapeDtypeStruct((rows // 2, width), BF16),
            jax.ShapeDtypeStruct((bags, width), F32),
        ),
        in_specs=[smem()] + [pl.BlockSpec(memory_space=pltpu.VMEM)] * 4,
        name="hot",
    )(side, hot_all, owner, hot_row, hot_bag)
    hot_got = lax.ppermute(hot_send, "tt", swap)

    (line_send,) = call(
        pair_kernel, "pair", (((pairs, slices + rows // 2, width), BF16),)
    )(keep, got, hot_keep, hot_got)
    lines = [list(range(c, tt_peers, 2)) for c in range(2)]
    line_got = lax.all_to_all(line_send, "tt", 0, 0, axis_index_groups=lines, tiled=True)

    (pooled,) = call(
        rows_kernel, "rows", (((bags, width), F32),),
        (((looks // LANES, width, LANES), F32), ((looks // LANES, width, LANES), F32)),
    )(first_all, maps, slice_owner, first_index, cold_bag, hot_part)

    cold_send, hot_half = call(
        line_kernel, "line", (((hot_peers, slices, width), BF16), ((rows // 2, width), F32))
    )(line_got)
    cold_got = lax.all_to_all(cold_send, "hot", 0, 0, tiled=True)
    hot_other = lax.ppermute(hot_half, "tt", swap)

    new_first, new_table, new_accum = pl.pallas_call(
        final_kernel,
        out_shape=(
            jax.ShapeDtypeStruct((slices, width), F32),
            jax.ShapeDtypeStruct((rows, width), F32),
            jax.ShapeDtypeStruct((1, rows), F32),
        ),
        in_specs=[smem()] + [pl.BlockSpec(memory_space=pltpu.VMEM)] * 6,
        name="final",
    )(side, cold_got, core_first, hot_half, hot_other, hot_table, hot_accum.reshape(1, -1))
    return pooled, new_table, new_accum.reshape(-1), new_first


def solution(mesh):
    both = P(("hot", "tt"), None)
    placed = (
        P("hot", None), P("hot"), both, both, both, both, both, both, both, both,
        P("tt", None), P(), P(), both,
    )
    return jax.shard_map(
        local,
        mesh=mesh,
        in_specs=placed,
        out_specs=(both, P("hot", None), P("hot"), P("tt", None)),
        check_vma=False,
    )
```

```python
import math

import jax
import jax.numpy as jnp
from jax import lax
from jax.experimental import pallas as pl
from jax.experimental.pallas import tpu as pltpu
from jax.sharding import PartitionSpec as P


E1 = 8
E2 = 8
E3 = 4
RANK = 32
TAIL = E2 * E3
LANES = 128
PAD = 16
FEW = 8
F32 = jnp.float32
BF16 = jnp.bfloat16
NT = (((1,), (1,)), ((), ()))


def iota(shape, dim):
    return lax.broadcasted_iota(jnp.int32, shape, dim)


def hot(mask):
    return mask.astype(F32).astype(BF16)


def mm(a, b):
    return jnp.dot(a, b, preferred_element_type=F32)


def mm_nt(a, b):
    return lax.dot_general(a, b, NT, preferred_element_type=F32)


def call(body, outs, args, scratch=(), far=0, spare=4 << 20):
    size = lambda shape, kind: math.prod(shape[:-2]) * max(shape[-2], 8) * max(shape[-1], LANES) * jnp.dtype(kind).itemsize
    scratch = tuple((x.shape, x.dtype) for x in args[:far]) + tuple(scratch)
    held = sum(size(a.shape, a.dtype) for a in args[far:]) + sum(size(*o) for o in tuple(outs) + scratch)
    near = len(args) - far

    def kernel(*refs):
        if not far:
            return body(*refs)
        given, rest, sem = refs[:far], refs[far:-1], refs[-1]
        taken = rest[near + len(outs) :]
        copies = [pltpu.make_async_copy(given[i], taken[i], sem.at[i]) for i in range(far)]
        for copy in copies:
            copy.start()
        for copy in copies:
            copy.wait()
        body(*taken[:far], *rest[: near + len(outs)], *taken[far:])

    args = [pltpu.with_memory_space_constraint(x, pltpu.HBM) for x in args[:far]] + list(args[far:])
    return pl.pallas_call(
        kernel,
        out_shape=tuple(jax.ShapeDtypeStruct(s, d) for s, d in outs),
        in_specs=[pl.BlockSpec(memory_space=pltpu.HBM)] * far + [pl.BlockSpec(memory_space=pltpu.VMEM)] * near,
        out_specs=(pl.BlockSpec(memory_space=pltpu.VMEM),) * len(outs),
        scratch_shapes=[pltpu.VMEM(s, d) for s, d in scratch]
        + ([pltpu.SemaphoreType.DMA((far,))] if far else []),
        compiler_params=pltpu.CompilerParams(vmem_limit_bytes=held + spare),
    )(*args)


def core_of():
    return lax.axis_index("tt") & 1


def tree(parts):
    while len(parts) > 1:
        parts = [parts[i] + parts[i + 1] for i in range(0, len(parts), 2)]
    return parts[0]


def swap(x, axis, bits):
    return lax.ppermute(x, axis, [(i, i ^ bits) for i in range(lax.axis_size(axis))])


def pack_kernel(table, grads, owner, row, bag, first, hot_out, first_out):
    rows, bags = table.shape[0], grads.shape[0]
    looks = jnp.concatenate(
        [owner[...], row[...], bag[...], jnp.zeros((PAD - 3, row.shape[1]), jnp.int32)], axis=0
    )
    turned = first[...].T.astype(BF16)
    for peer in range(hot_out.shape[0]):
        hot_out[peer, 0:rows, :] = table[...].astype(BF16)
        hot_out[peer, rows : rows + bags, :] = grads[...]
        hot_out[peer, rows + bags :, :] = looks.astype(F32).astype(BF16)
    for peer in range(first_out.shape[0]):
        first_out[peer] = turned


def maps_kernel(
    mid, last, mid_index, last_index, bag, owner, index, grads,
    keep, send, maps, keys, turned, left, right, lasts_of, cot, terms,
):
    mids, lasts = mid.shape[0], last.shape[0]
    looks = bag.shape[1]

    def turn(t, _):
        at = pl.ds(pl.multiple_of(t * LANES, LANES), LANES)
        block = mid[:, at].astype(F32)
        turned[at, :] = jnp.concatenate([block, block], axis=0).T
        return 0

    lax.fori_loop(0, mid.shape[1] // LANES, turn, 0, unroll=4)
    first_half = iota((RANK * E2, 2 * mids), 1) < mids
    for pair in range(RANK // 2):
        low = turned[pl.ds(2 * pair, RANK * E2, stride=RANK), :]
        high = turned[pl.ds(2 * pair + 1, RANK * E2, stride=RANK), :]
        left[:, pair * 2 * mids : (pair + 1) * 2 * mids] = jnp.where(first_half, low, high).astype(BF16)
    pick_last = hot(iota((lasts, looks), 0) == last_index[...])
    lasts_of[...] = mm(last[...].astype(F32).T.astype(BF16), pick_last)
    pick_bag = hot(iota((grads.shape[0], looks), 0) == bag[...])
    cot[...] = mm(grads[...].astype(F32).T.astype(BF16), pick_bag)
    pick_mid = hot(iota((mids, looks), 0) == mid_index[...])
    for e3 in range(E3):
        for b in range(RANK):
            at = b * E3 + e3
            spread = jnp.broadcast_to(lasts_of[at : at + 1, :], (PAD, looks)).astype(BF16)
            for part in range(0, mids, PAD):
                right[b * mids + part : b * mids + part + PAD, :] = pick_mid[part : part + PAD, :] * spread
        made = mm(left[...], right[...]).astype(BF16).astype(F32)
        for t in range(looks // LANES):
            maps[t, e3 * RANK * E2 : (e3 + 1) * RANK * E2, :] = made[:, t * LANES : (t + 1) * LANES]

    def back(t, _):
        lanes = pl.ds(pl.multiple_of(t * LANES, LANES), LANES)
        sums = [jnp.zeros((RANK, LANES), F32) for _ in range(E1)]
        for e2 in range(E2):
            for e3 in range(E3):
                part = maps[t, pl.ds(e3 * RANK * E2 + e2, RANK, stride=E2), :]
                for e1 in range(E1):
                    at = e1 * TAIL + e2 * E3 + e3
                    sums[e1] = sums[e1] + part * cot[at : at + 1, lanes]
        for e1 in range(E1):
            terms[e1 * RANK : (e1 + 1) * RANK, lanes] = sums[e1]
        return 0

    lax.fori_loop(0, looks // LANES, back, 0)
    whole = terms[...]
    high = whole.astype(BF16)
    low = (whole - high.astype(F32)).astype(BF16)
    own = owner[...]
    held = keep.shape[0]
    slices = held // (lax.axis_size("tt") // 2)
    key = ((own & 1) ^ core_of()) * held + (own >> 1) * slices + index[...]
    step = min(held, 256)
    keys[0:1, :] = own * slices + index[...]
    keys[1:2, :] = bag[...]
    for half, out in ((0, keep), (1, send)):
        for start in range(0, held, step):
            pick = hot(iota((step, looks), 0) + (half * held + start) == key)
            out[start : start + step, :] = (mm_nt(pick, high) + mm_nt(pick, low)).astype(out.dtype)


def hot_kernel(*refs):
    gathered, (keep, send, pooled) = refs[:-3], refs[-3:]
    me = lax.axis_index("hot")
    if len(gathered) > 1:
        sources = [(me ^ bits, part.at[0]) for bits, part in enumerate(gathered)]
        mine = gathered[0].at[0]
    else:
        sources = [(peer, gathered[0].at[peer]) for peer in range(gathered[0].shape[0])]
        mine = gathered[0].at[me]
    bags = pooled.shape[0]
    half = keep.shape[0]
    rows = 2 * half

    def lookups(part):
        sent = part[rows + bags :, :].astype(F32).astype(jnp.int32)
        return sent[0:1, :], sent[1:2, :], sent[2:3, :]

    owner, row, bag = lookups(mine)
    looks = row.shape[1]
    at = iota((rows, looks), 0)
    pick_bag = hot(iota((bags, looks), 0) == bag)
    total = jnp.zeros(pooled.shape, F32)
    for peer, part in sources:
        pick = hot((at == row) & (owner == peer))
        total = total + mm(mm_nt(pick_bag, pick).astype(BF16), part[0:rows, :])
    pooled[...] = total
    grad = jnp.zeros((rows, pooled.shape[1]), F32)
    for peer, part in sources:
        theirs, place, their_bag = lookups(part)
        upper = (place >= half).astype(jnp.int32)
        place = (upper ^ core_of()) * half + place - upper * half
        pick = hot((at == place) & (theirs == me))
        count = mm_nt(pick, hot(iota((bags, looks), 0) == their_bag))
        grad = grad + mm(count.astype(BF16), part[rows : rows + bags, :])
    keep[...] = grad[0:half]
    send[...] = grad[half:].astype(BF16)


def pair_kernel(cold_keep, cold_got, hot_keep, hot_got, own, *sends):
    slices = cold_keep.shape[0] // (1 + len(sends))
    place = lax.axis_index("tt") >> 1
    hot_sum = (hot_keep[...] + hot_got[...].astype(F32)).astype(BF16)
    for bits, out in enumerate((own,) + sends):
        at = pl.ds(pl.multiple_of((place ^ bits) * slices, slices), slices)
        out[0:slices, :] = (cold_keep[at, :] + cold_got[at, :].astype(F32)).astype(BF16)
        out[slices:, :] = hot_sum


def line_kernel(*refs):
    cold, hot_half = refs[-2:]
    slices = cold.shape[1]
    total = tree([part[...].astype(F32) for part in refs[:-2]])
    sent = total[0:slices].astype(BF16)
    for peer in range(cold.shape[0]):
        cold[peer] = sent
    hot_half[...] = total[slices:]


def rows_kernel(gathered, maps, keys, hot_part, pooled, slices_of, rows):
    peers, width, slices = gathered.shape
    looks = keys.shape[1]
    tiles = looks // LANES
    key = keys[0:1, :]
    total = jnp.zeros((width, looks), F32)
    for peer in range(peers):
        pick = hot(iota((slices, looks), 0) + peer * slices == key)
        total = total + mm(gathered[peer], pick)
    for t in range(tiles):
        slices_of[t] = total[:, t * LANES : (t + 1) * LANES]

    def forward(t, _):
        sums = [[jnp.zeros((E2, LANES), F32) for _ in range(E3)] for _ in range(E1)]
        for a in range(RANK):
            parts = [maps[t, e3 * RANK * E2 + a * E2 : e3 * RANK * E2 + a * E2 + E2, :] for e3 in range(E3)]
            for e1 in range(E1):
                entry = slices_of[t, e1 * RANK + a : e1 * RANK + a + 1, :]
                for e3 in range(E3):
                    sums[e1][e3] = sums[e1][e3] + parts[e3] * entry
        for e1 in range(E1):
            for e3 in range(E3):
                rows[t, pl.ds(e1 * TAIL + e3, E2, stride=E3), :] = sums[e1][e3]
        return 0

    lax.fori_loop(0, tiles, forward, 0)
    out = hot_part[...]
    for t in range(tiles):
        pick = hot(iota((pooled.shape[0], LANES), 0) == keys[1:2, t * LANES : (t + 1) * LANES])
        out = out + mm_nt(pick, rows[t].astype(BF16))
    pooled[...] = out


def final_kernel(first, mine, other, table, accum, *refs):
    parts, (new_first, new_table, new_accum) = refs[:-3], refs[-3:]
    total = tree([part[peer].astype(F32) for part in parts for peer in range(part.shape[0])])
    new_first[...] = first[...] - 0.01 * total
    lower = core_of() == 0
    grad = jnp.concatenate(
        [jnp.where(lower, mine[...], other[...]), jnp.where(lower, other[...], mine[...])], axis=0
    )
    rows = grad.shape[0]
    mean = jnp.mean(grad * grad, axis=1, keepdims=True)
    held = jnp.broadcast_to(accum[...], (LANES, rows)).T + mean
    new_accum[...] = held.T[0:1, :]
    new_table[...] = table[...] - 0.1 * grad / (jnp.sqrt(held[:, 0:1]) + 1e-08)


def local(
    hot_table, hot_accum, hot_owner, hot_row, hot_bag, cold_owner, first_index,
    mid_index, last_index, cold_bag, core_first, core_mid, core_last, bag_grads,
):
    rows, width = hot_table.shape
    bags = bag_grads.shape[0]
    slices = core_first.shape[0]
    hot_peers, tt_peers = lax.axis_size("hot"), lax.axis_size("tt")
    pairs = tt_peers // 2
    looks = cold_bag.shape[1]
    assert max(rows, bags, hot_peers) <= 256
    owner = hot_owner.reshape(1, -1)
    slice_owner = cold_owner.reshape(1, -1)
    held = slices * pairs
    few = hot_peers <= FEW
    tiles = looks // LANES

    hot_pack, first_pack = call(
        pack_kernel,
        (((1 if few else hot_peers, rows + bags + PAD, width), BF16), ((tt_peers, width, slices), BF16)),
        (hot_table, bag_grads, owner, hot_row, hot_bag, core_first),
        far=6,
    )

    def spread(x):
        if few:
            out = [x]
            for bits in range(1, hot_peers):
                out.append(swap(x, "hot", bits))
            return out
        return [lax.all_to_all(x, "hot", 0, 0, tiled=True)]

    hot_all = spread(hot_pack)
    first_all = lax.all_to_all(first_pack, "tt", 0, 0, tiled=True)

    keep, send, maps, keys = call(
        maps_kernel,
        (((held, width), F32), ((held, width), BF16), ((tiles, E3 * RANK * E2, LANES), F32), ((8, looks), jnp.int32)),
        (core_mid, core_last, mid_index, last_index, cold_bag, slice_owner, first_index, bag_grads),
        (
            ((core_mid.shape[1], LANES), F32),
            ((RANK * E2, RANK * core_mid.shape[0]), BF16),
            ((RANK * core_mid.shape[0], looks), BF16),
            ((RANK * E3, looks), F32),
            ((width, looks), F32),
            ((width, looks), F32),
        ),
        far=8,
    )
    got = swap(send, "tt", 1)

    hot_keep, hot_send, hot_part = call(
        hot_kernel, (((rows // 2, width), F32), ((rows // 2, width), BF16), ((bags, width), F32)), hot_all
    )
    hot_got = swap(hot_send, "tt", 1)

    pieces = call(
        pair_kernel, (((slices + rows // 2, width), BF16),) * pairs,
        (keep, got, hot_keep, hot_got),
    )
    parts = [pieces[0]]
    for bits in range(1, pairs):
        parts.append(swap(pieces[bits], "tt", 2 * bits))

    (pooled,) = call(
        rows_kernel, (((bags, width), F32),),
        (first_all, maps, keys, hot_part),
        (((tiles, width, LANES), F32), ((tiles, width, LANES), F32)),
    )

    cold_send, hot_half = call(
        line_kernel, (((1 if few else hot_peers, slices, width), BF16), ((rows // 2, width), F32)), parts
    )
    cold_all = spread(cold_send)
    hot_other = swap(hot_half, "tt", 1)

    new_first, new_table, new_accum = call(
        final_kernel,
        (((slices, width), F32), ((rows, width), F32), ((1, rows), F32)),
        (core_first, hot_half, hot_other, hot_table, hot_accum.reshape(1, -1), *cold_all),
    )
    return pooled, new_table, new_accum.reshape(-1), new_first


def solution(mesh):
    both = P(("hot", "tt"), None)
    placed = (
        P("hot", None), P("hot"), both, both, both, both, both, both, both, both,
        P("tt", None), P(), P(), both,
    )

    return jax.shard_map(
        local,
        mesh=mesh,
        in_specs=placed,
        out_specs=(both, P("hot", None), P("hot"), P("tt", None)),
        check_vma=False,
    )
```

```python
import math

import jax
import jax.numpy as jnp
from jax import lax
from jax.experimental import pallas as pl
from jax.experimental.pallas import tpu as pltpu
from jax.sharding import PartitionSpec as P


E1 = 8
E2 = 8
E3 = 4
RANK = 32
TAIL = E2 * E3
LANES = 128
PAD = 16
FEW = 8
F32 = jnp.float32
BF16 = jnp.bfloat16
NT = (((1,), (1,)), ((), ()))


def iota(shape, dim):
    return lax.broadcasted_iota(jnp.int32, shape, dim)


def hot(mask):
    return mask.astype(F32).astype(BF16)


def mm(a, b):
    return jnp.dot(a, b, preferred_element_type=F32)


def mm_nt(a, b):
    return lax.dot_general(a, b, NT, preferred_element_type=F32)


def call(body, outs, args, scratch=(), far=0, spare=4 << 20):
    size = lambda shape, kind: math.prod(shape[:-2]) * max(shape[-2], 8) * max(shape[-1], LANES) * jnp.dtype(kind).itemsize
    scratch = tuple((x.shape, x.dtype) for x in args[:far]) + tuple(scratch)
    held = sum(size(a.shape, a.dtype) for a in args[far:]) + sum(size(*o) for o in tuple(outs) + scratch)
    near = len(args) - far

    def kernel(*refs):
        if not far:
            return body(*refs)
        given, rest, sem = refs[:far], refs[far:-1], refs[-1]
        taken = rest[near + len(outs) :]
        copies = [pltpu.make_async_copy(given[i], taken[i], sem.at[i]) for i in range(far)]
        for copy in copies:
            copy.start()
        for copy in copies:
            copy.wait()
        body(*taken[:far], *rest[: near + len(outs)], *taken[far:])

    args = [pltpu.with_memory_space_constraint(x, pltpu.HBM) for x in args[:far]] + list(args[far:])
    return pl.pallas_call(
        kernel,
        out_shape=tuple(jax.ShapeDtypeStruct(s, d) for s, d in outs),
        in_specs=[pl.BlockSpec(memory_space=pltpu.HBM)] * far + [pl.BlockSpec(memory_space=pltpu.VMEM)] * near,
        out_specs=(pl.BlockSpec(memory_space=pltpu.VMEM),) * len(outs),
        scratch_shapes=[pltpu.VMEM(s, d) for s, d in scratch]
        + ([pltpu.SemaphoreType.DMA((far,))] if far else []),
        compiler_params=pltpu.CompilerParams(vmem_limit_bytes=held + spare),
    )(*args)


def core_of():
    return lax.axis_index("tt") & 1


def tree(parts):
    while len(parts) > 1:
        parts = [parts[i] + parts[i + 1] for i in range(0, len(parts), 2)]
    return parts[0]


def swap(x, axis, bits):
    return lax.ppermute(x, axis, [(i, i ^ bits) for i in range(lax.axis_size(axis))])


def pack_kernel(table, grads, owner, row, bag, first, hot_out, first_out):
    rows, bags = table.shape[0], grads.shape[0]
    looks = jnp.concatenate(
        [owner[...], row[...], bag[...], jnp.zeros((PAD - 3, row.shape[1]), jnp.int32)], axis=0
    )
    turned = first[...].T.astype(BF16)
    for peer in range(hot_out.shape[0]):
        hot_out[peer, 0:rows, :] = table[...].astype(BF16)
        hot_out[peer, rows : rows + bags, :] = grads[...]
        hot_out[peer, rows + bags :, :] = looks.astype(F32).astype(BF16)
    first_out[...] = turned


def maps_kernel(
    mid, last, mid_index, last_index, bag, owner, index, grads,
    keep, send, maps, keys, turned, left, right, lasts_of, cot, terms,
):
    mids, lasts = mid.shape[0], last.shape[0]
    looks = bag.shape[1]

    def turn(t, _):
        at = pl.ds(pl.multiple_of(t * LANES, LANES), LANES)
        block = mid[:, at].astype(F32)
        turned[at, :] = jnp.concatenate([block, block], axis=0).T
        return 0

    lax.fori_loop(0, mid.shape[1] // LANES, turn, 0, unroll=4)
    first_half = iota((RANK * E2, 2 * mids), 1) < mids
    for pair in range(RANK // 2):
        low = turned[pl.ds(2 * pair, RANK * E2, stride=RANK), :]
        high = turned[pl.ds(2 * pair + 1, RANK * E2, stride=RANK), :]
        left[:, pair * 2 * mids : (pair + 1) * 2 * mids] = jnp.where(first_half, low, high).astype(BF16)
    pick_last = hot(iota((lasts, looks), 0) == last_index[...])
    lasts_of[...] = mm(last[...].astype(F32).T.astype(BF16), pick_last)
    pick_bag = hot(iota((grads.shape[0], looks), 0) == bag[...])
    cot[...] = mm(grads[...].astype(F32).T.astype(BF16), pick_bag)
    pick_mid = hot(iota((mids, looks), 0) == mid_index[...])
    for e3 in range(E3):
        for b in range(RANK):
            at = b * E3 + e3
            spread = jnp.broadcast_to(lasts_of[at : at + 1, :], (PAD, looks)).astype(BF16)
            for part in range(0, mids, PAD):
                right[b * mids + part : b * mids + part + PAD, :] = pick_mid[part : part + PAD, :] * spread
        made = mm(left[...], right[...]).astype(BF16).astype(F32)
        for t in range(looks // LANES):
            maps[t, e3 * RANK * E2 : (e3 + 1) * RANK * E2, :] = made[:, t * LANES : (t + 1) * LANES]

    def back(t, _):
        lanes = pl.ds(pl.multiple_of(t * LANES, LANES), LANES)
        sums = [jnp.zeros((RANK, LANES), F32) for _ in range(E1)]
        for e2 in range(E2):
            for e3 in range(E3):
                part = maps[t, pl.ds(e3 * RANK * E2 + e2, RANK, stride=E2), :]
                for e1 in range(E1):
                    at = e1 * TAIL + e2 * E3 + e3
                    sums[e1] = sums[e1] + part * cot[at : at + 1, lanes]
        for e1 in range(E1):
            terms[e1 * RANK : (e1 + 1) * RANK, lanes] = sums[e1]
        return 0

    lax.fori_loop(0, looks // LANES, back, 0)
    whole = terms[...]
    high = whole.astype(BF16)
    low = (whole - high.astype(F32)).astype(BF16)
    own = owner[...]
    held = keep.shape[0]
    slices = held // (lax.axis_size("tt") // 2)
    key = ((own & 1) ^ core_of()) * held + (own >> 1) * slices + index[...]
    step = min(held, 256)
    keys[0:1, :] = own * slices + index[...]
    keys[1:2, :] = bag[...]
    for half, out in ((0, keep), (1, send)):
        for start in range(0, held, step):
            pick = hot(iota((step, looks), 0) + (half * held + start) == key)
            out[start : start + step, :] = (mm_nt(pick, high) + mm_nt(pick, low)).astype(out.dtype)


def hot_kernel(*refs):
    gathered, (keep, send, pooled) = refs[:-3], refs[-3:]
    me = lax.axis_index("hot")
    if len(gathered) > 1:
        sources = [(me ^ bits, part.at[0]) for bits, part in enumerate(gathered)]
        mine = gathered[0].at[0]
    else:
        sources = [(peer, gathered[0].at[peer]) for peer in range(gathered[0].shape[0])]
        mine = gathered[0].at[me]
    bags = pooled.shape[0]
    half = keep.shape[0]
    rows = 2 * half

    def lookups(part):
        sent = part[rows + bags :, :].astype(F32).astype(jnp.int32)
        return sent[0:1, :], sent[1:2, :], sent[2:3, :]

    owner, row, bag = lookups(mine)
    looks = row.shape[1]
    at = iota((rows, looks), 0)
    pick_bag = hot(iota((bags, looks), 0) == bag)
    total = jnp.zeros(pooled.shape, F32)
    for peer, part in sources:
        pick = hot((at == row) & (owner == peer))
        total = total + mm(mm_nt(pick_bag, pick).astype(BF16), part[0:rows, :])
    pooled[...] = total
    grad = jnp.zeros((rows, pooled.shape[1]), F32)
    for peer, part in sources:
        theirs, place, their_bag = lookups(part)
        upper = (place >= half).astype(jnp.int32)
        place = (upper ^ core_of()) * half + place - upper * half
        pick = hot((at == place) & (theirs == me))
        count = mm_nt(pick, hot(iota((bags, looks), 0) == their_bag))
        grad = grad + mm(count.astype(BF16), part[rows : rows + bags, :])
    keep[...] = grad[0:half]
    send[...] = grad[half:].astype(BF16)


def pair_kernel(cold_keep, cold_got, hot_keep, hot_got, own, *sends):
    slices = own.shape[0]
    place = lax.axis_index("tt") >> 1
    for bits, out in enumerate((own,) + sends):
        at = pl.ds(pl.multiple_of((place ^ bits) * slices, slices), slices)
        out[0:slices, :] = (cold_keep[at, :] + cold_got[at, :].astype(F32)).astype(BF16)
    sends[0][slices:, :] = (hot_keep[...] + hot_got[...].astype(F32)).astype(BF16)


def step_kernel(mine, got, total):
    rows = total.shape[0]
    total[...] = (
        mine[mine.shape[0] - rows :, :].astype(F32) + got[got.shape[0] - rows :, :].astype(F32)
    ).astype(total.dtype)


def line_kernel(*refs):
    parts, cold = refs[:-1], refs[-1]
    slices = cold.shape[1]
    sent = tree([part[0:slices, :].astype(F32) for part in parts]).astype(BF16)
    for peer in range(cold.shape[0]):
        cold[peer] = sent


def rows_kernel(maps, keys, hot_part, *refs):
    gathered, (pooled, slices_of, rows) = refs[:-3], refs[-3:]
    width, slices = gathered[0].shape
    me = lax.axis_index("tt")
    looks = keys.shape[1]
    tiles = looks // LANES
    key = keys[0:1, :]
    total = jnp.zeros((width, looks), F32)
    for bits, part in enumerate(gathered):
        pick = hot(iota((slices, looks), 0) + (me ^ bits) * slices == key)
        total = total + mm(part[...], pick)
    for t in range(tiles):
        slices_of[t] = total[:, t * LANES : (t + 1) * LANES]

    def forward(t, _):
        sums = [[jnp.zeros((E2, LANES), F32) for _ in range(E3)] for _ in range(E1)]
        for a in range(RANK):
            parts = [maps[t, e3 * RANK * E2 + a * E2 : e3 * RANK * E2 + a * E2 + E2, :] for e3 in range(E3)]
            for e1 in range(E1):
                entry = slices_of[t, e1 * RANK + a : e1 * RANK + a + 1, :]
                for e3 in range(E3):
                    sums[e1][e3] = sums[e1][e3] + parts[e3] * entry
        for e1 in range(E1):
            for e3 in range(E3):
                rows[t, pl.ds(e1 * TAIL + e3, E2, stride=E3), :] = sums[e1][e3]
        return 0

    lax.fori_loop(0, tiles, forward, 0)
    out = hot_part[...]
    for t in range(tiles):
        pick = hot(iota((pooled.shape[0], LANES), 0) == keys[1:2, t * LANES : (t + 1) * LANES])
        out = out + mm_nt(pick, rows[t].astype(BF16))
    pooled[...] = out


def final_kernel(first, mine, other, table, accum, *refs):
    parts, (new_first, new_table, new_accum) = refs[:-3], refs[-3:]
    total = tree([part[peer].astype(F32) for part in parts for peer in range(part.shape[0])])
    new_first[...] = first[...] - 0.01 * total
    lower = core_of() == 0
    grad = jnp.concatenate(
        [jnp.where(lower, mine[...], other[...]), jnp.where(lower, other[...], mine[...])], axis=0
    )
    rows = grad.shape[0]
    mean = jnp.mean(grad * grad, axis=1, keepdims=True)
    held = jnp.broadcast_to(accum[...], (LANES, rows)).T + mean
    new_accum[...] = held.T[0:1, :]
    new_table[...] = table[...] - 0.1 * grad / (jnp.sqrt(held[:, 0:1]) + 1e-08)


def local(
    hot_table, hot_accum, hot_owner, hot_row, hot_bag, cold_owner, first_index,
    mid_index, last_index, cold_bag, core_first, core_mid, core_last, bag_grads,
):
    rows, width = hot_table.shape
    bags = bag_grads.shape[0]
    slices = core_first.shape[0]
    hot_peers, tt_peers = lax.axis_size("hot"), lax.axis_size("tt")
    pairs = tt_peers // 2
    looks = cold_bag.shape[1]
    assert max(rows, bags, hot_peers) <= 256
    owner = hot_owner.reshape(1, -1)
    slice_owner = cold_owner.reshape(1, -1)
    held = slices * pairs
    few = hot_peers <= FEW
    tiles = looks // LANES

    hot_pack, first_pack = call(
        pack_kernel,
        (((1 if few else hot_peers, rows + bags + PAD, width), BF16), ((width, slices), BF16)),
        (hot_table, bag_grads, owner, hot_row, hot_bag, core_first),
        far=6,
    )

    def spread(x):
        if few:
            out = [x]
            for bits in range(1, hot_peers):
                out.append(swap(x, "hot", bits))
            return out
        return [lax.all_to_all(x, "hot", 0, 0, tiled=True)]

    hot_all = spread(hot_pack)
    keep, send, maps, keys = call(
        maps_kernel,
        (((held, width), F32), ((held, width), BF16), ((tiles, E3 * RANK * E2, LANES), F32), ((8, looks), jnp.int32)),
        (core_mid, core_last, mid_index, last_index, cold_bag, slice_owner, first_index, bag_grads),
        (
            ((core_mid.shape[1], LANES), F32),
            ((RANK * E2, RANK * core_mid.shape[0]), BF16),
            ((RANK * core_mid.shape[0], looks), BF16),
            ((RANK * E3, looks), F32),
            ((width, looks), F32),
            ((width, looks), F32),
        ),
        far=8,
    )
    got = swap(send, "tt", 1)

    hot_keep, hot_send, hot_part = call(
        hot_kernel, (((rows // 2, width), F32), ((rows // 2, width), BF16), ((bags, width), F32)), hot_all
    )
    hot_got = swap(hot_send, "tt", 1)

    half = rows // 2
    pieces = call(
        pair_kernel,
        tuple(((slices + (half if bits == 1 else 0), width), BF16) for bits in range(pairs)),
        (keep, got, hot_keep, hot_got),
    )
    parts = [pieces[0]]
    for bits in range(1, pairs):
        parts.append(swap(pieces[bits], "tt", 2 * bits))

    shards = [first_pack]
    for bits in range(1, pairs):
        shards.append(swap(first_pack, "tt", 2 * bits))
    first_all = []
    for bits, shard in enumerate(shards):
        first_all += [shard, swap(shard, "tt", 1)]

    mine, theirs, bits = pieces[1], parts[1], 2
    while bits < pairs:
        (mine,) = call(step_kernel, (((half, width), BF16),), (mine, theirs))
        theirs = swap(mine, "tt", 2 * bits)
        bits *= 2
    (hot_half,) = call(step_kernel, (((half, width), F32),), (mine, theirs))
    hot_other = swap(hot_half, "tt", 1)

    (cold_send,) = call(line_kernel, (((1 if few else hot_peers, slices, width), BF16),), parts)
    cold_all = spread(cold_send)

    (pooled,) = call(
        rows_kernel, (((bags, width), F32),),
        (maps, keys, hot_part, *first_all),
        (((tiles, width, LANES), F32), ((tiles, width, LANES), F32)),
    )

    new_first, new_table, new_accum = call(
        final_kernel,
        (((slices, width), F32), ((rows, width), F32), ((1, rows), F32)),
        (core_first, hot_half, hot_other, hot_table, hot_accum.reshape(1, -1), *cold_all),
    )
    return pooled, new_table, new_accum.reshape(-1), new_first


def solution(mesh):
    both = P(("hot", "tt"), None)
    placed = (
        P("hot", None), P("hot"), both, both, both, both, both, both, both, both,
        P("tt", None), P(), P(), both,
    )

    return jax.shard_map(
        local,
        mesh=mesh,
        in_specs=placed,
        out_specs=(both, P("hot", None), P("hot"), P("tt", None)),
        check_vma=False,
    )
```

```python
import functools
import math

import jax
import jax.numpy as jnp
from jax import lax
from jax.experimental import pallas as pl
from jax.experimental.pallas import tpu as pltpu
from jax.sharding import PartitionSpec as P


E1 = 8
E2 = 8
E3 = 4
RANK = 32
TAIL = E2 * E3
LANES = 128
PAD = 16
PITCH = RANK + 1
FEW = 8
F32 = jnp.float32
BF16 = jnp.bfloat16
NT = (((1,), (1,)), ((), ()))


def iota(shape, dim):
    return lax.broadcasted_iota(jnp.int32, shape, dim)


def hot(mask):
    return mask.astype(F32).astype(BF16)


def mm(a, b):
    return jnp.dot(a, b, preferred_element_type=F32)


def mm_nt(a, b):
    return lax.dot_general(a, b, NT, preferred_element_type=F32)


def call(body, outs, args, scratch=(), far=0, spare=4 << 20):
    size = lambda shape, kind: math.prod(shape[:-2]) * max(shape[-2], 8) * max(shape[-1], LANES) * jnp.dtype(kind).itemsize
    scratch = tuple((x.shape, x.dtype) for x in args[:far]) + tuple(scratch)
    held = sum(size(a.shape, a.dtype) for a in args[far:]) + sum(size(*o) for o in tuple(outs) + scratch)
    near = len(args) - far

    def kernel(*refs):
        if not far:
            return body(*refs)
        given, rest, sem = refs[:far], refs[far:-1], refs[-1]
        taken = rest[near + len(outs) :]
        copies = [pltpu.make_async_copy(given[i], taken[i], sem.at[i]) for i in range(far)]
        for copy in copies:
            copy.start()
        for copy in copies:
            copy.wait()
        body(*taken[:far], *rest[: near + len(outs)], *taken[far:])

    args = [pltpu.with_memory_space_constraint(x, pltpu.HBM) for x in args[:far]] + list(args[far:])
    return pl.pallas_call(
        kernel,
        out_shape=tuple(jax.ShapeDtypeStruct(s, d) for s, d in outs),
        in_specs=[pl.BlockSpec(memory_space=pltpu.HBM)] * far + [pl.BlockSpec(memory_space=pltpu.VMEM)] * near,
        out_specs=(pl.BlockSpec(memory_space=pltpu.VMEM),) * len(outs),
        scratch_shapes=[pltpu.VMEM(s, d) for s, d in scratch]
        + ([pltpu.SemaphoreType.DMA((far,))] if far else []),
        compiler_params=pltpu.CompilerParams(vmem_limit_bytes=held + spare),
    )(*args)


def core_of():
    return lax.axis_index("tt") & 1


def tree(parts):
    while len(parts) > 1:
        parts = [parts[i] + parts[i + 1] for i in range(0, len(parts), 2)]
    return parts[0]


def swap(x, axis, bits):
    return lax.ppermute(x, axis, [(i, i ^ bits) for i in range(lax.axis_size(axis))])


def pack_kernel(table, grads, owner, row, bag, first, *refs):
    count = len(refs) // 2 - 1
    hot_out, first_out = refs[count : count + 2]
    for src, dst in zip((grads,) + refs[:count], refs[count + 2 :]):
        dst[...] = src[...]
    rows, bags = table.shape[0], grads.shape[0]
    lower = first_out.shape[0]
    looks = jnp.concatenate(
        [owner[...], row[...], bag[...], jnp.zeros((PAD - 3, row.shape[1]), jnp.int32)], axis=0
    )
    turned = first[...].T.astype(BF16)
    for peer in range(hot_out.shape[0]):
        hot_out[peer, 0:rows, :] = table[...].astype(BF16)
        hot_out[peer, rows : rows + bags, :] = grads[...]
        hot_out[peer, rows + bags :, :] = looks.astype(F32).astype(BF16)
    first_out[...] = jnp.concatenate([turned[0:lower], turned[lower:]], axis=1)


def maps_kernel(
    mid, last, mid_index, last_index, bag, owner, index, grads,
    keep, send, maps, keys, turned, left, right, lasts_of, cot, terms,
):
    mids, lasts = mid.shape[0], last.shape[0]
    looks = bag.shape[1]

    def turn(t, _):
        at = pl.ds(pl.multiple_of(t * LANES, LANES), LANES)
        block = mid[:, at].astype(F32)
        block = jnp.concatenate([block, block], axis=0).T
        for part in range(LANES // RANK):
            turned[pl.ds((t * (LANES // RANK) + part) * PITCH, RANK), :] = block[part * RANK : (part + 1) * RANK, :]
        return 0

    lax.fori_loop(0, mid.shape[1] // LANES, turn, 0, unroll=4)
    first_half = iota((RANK * E2, 2 * mids), 1) < mids
    for pair in range(RANK // 2):
        low = turned[pl.ds(2 * pair, RANK * E2, stride=PITCH), :]
        high = turned[pl.ds(2 * pair + 1, RANK * E2, stride=PITCH), :]
        left[:, pair * 2 * mids : (pair + 1) * 2 * mids] = jnp.where(first_half, low, high).astype(BF16)
    pick_last = hot(iota((lasts, looks), 0) == last_index[...])
    lasts_of[...] = mm(last[...].astype(F32).T.astype(BF16), pick_last)
    pick_bag = hot(iota((grads.shape[0], looks), 0) == bag[...])
    cot[...] = mm(grads[...].astype(F32).T.astype(BF16), pick_bag)
    pick_mid = hot(iota((mids, looks), 0) == mid_index[...])
    for e3 in range(E3):
        for b in range(RANK):
            at = b * E3 + e3
            spread = jnp.broadcast_to(lasts_of[at : at + 1, :], (PAD, looks)).astype(BF16)
            for part in range(0, mids, PAD):
                right[b * mids + part : b * mids + part + PAD, :] = pick_mid[part : part + PAD, :] * spread
        made = mm(left[...], right[...]).astype(BF16).astype(F32)
        for t in range(looks // LANES):
            maps[t, e3 * RANK * E2 : (e3 + 1) * RANK * E2, :] = made[:, t * LANES : (t + 1) * LANES]

    def back(t, _):
        lanes = pl.ds(pl.multiple_of(t * LANES, LANES), LANES)
        sums = [jnp.zeros((RANK, LANES), F32) for _ in range(E1)]
        for e2 in range(E2):
            for e3 in range(E3):
                part = maps[t, pl.ds(e3 * RANK * E2 + e2, RANK, stride=E2), :]
                for e1 in range(E1):
                    at = e1 * TAIL + e2 * E3 + e3
                    sums[e1] = sums[e1] + part * cot[at : at + 1, lanes]
        for e1 in range(E1):
            terms[e1 * RANK : (e1 + 1) * RANK, lanes] = sums[e1]
        return 0

    lax.fori_loop(0, looks // LANES, back, 0)
    whole = terms[...].astype(BF16)
    own = owner[...]
    held = keep.shape[0]
    slices = held // (lax.axis_size("tt") // 2)
    key = ((own & 1) ^ core_of()) * held + (own >> 1) * slices + index[...]
    step = min(held, 256)
    keys[0:1, :] = own * slices + index[...]
    keys[1:2, :] = bag[...]
    for half, out in ((0, keep), (1, send)):
        for start in range(0, held, step):
            pick = hot(iota((step, looks), 0) + (half * held + start) == key)
            out[start : start + step, :] = mm_nt(pick, whole).astype(out.dtype)


def hot_kernel(*refs):
    gathered, (keep, send, pooled) = refs[:-3], refs[-3:]
    me = lax.axis_index("hot")
    if len(gathered) > 1:
        sources = [(me ^ bits, part.at[0]) for bits, part in enumerate(gathered)]
        mine = gathered[0].at[0]
    else:
        sources = [(peer, gathered[0].at[peer]) for peer in range(gathered[0].shape[0])]
        mine = gathered[0].at[me]
    bags = pooled.shape[0]
    half = keep.shape[0]
    rows = 2 * half

    def lookups(part):
        sent = part[rows + bags :, :].astype(F32).astype(jnp.int32)
        return sent[0:1, :], sent[1:2, :], sent[2:3, :]

    owner, row, bag = lookups(mine)
    looks = row.shape[1]
    at = iota((rows, looks), 0)
    pick_bag = hot(iota((bags, looks), 0) == bag)
    total = jnp.zeros(pooled.shape, F32)
    for peer, part in sources:
        pick = hot((at == row) & (owner == peer))
        total = total + mm(mm_nt(pick_bag, pick).astype(BF16), part[0:rows, :])
    pooled[...] = total
    grad = jnp.zeros((rows, pooled.shape[1]), F32)
    for peer, part in sources:
        theirs, place, their_bag = lookups(part)
        upper = (place >= half).astype(jnp.int32)
        place = (upper ^ core_of()) * half + place - upper * half
        pick = hot((at == place) & (theirs == me))
        count = mm_nt(pick, hot(iota((bags, looks), 0) == their_bag))
        grad = grad + mm(count.astype(BF16), part[rows : rows + bags, :])
    keep[...] = grad[0:half]
    send[...] = grad[half:].astype(BF16)


def pair_kernel(pairs, cold_keep, cold_got, hot_keep, hot_got, *refs):
    shards, (held, own, *sends) = refs[:-1 - pairs], refs[-1 - pairs :]
    slices = own.shape[0]
    place = lax.axis_index("tt") >> 1
    for bits, out in enumerate((own, *sends)):
        at = pl.ds(pl.multiple_of((place ^ bits) * slices, slices), slices)
        out[0:slices, :] = (cold_keep[at, :] + cold_got[at, :].astype(F32)).astype(BF16)
    sends[0][slices:, :] = (hot_keep[...] + hot_got[...].astype(F32)).astype(BF16)
    for i, shard in enumerate(shards):
        held[i * slices : (i + 1) * slices, :] = shard[...]


def step_kernel(at, mine, got, total):
    total[...] = (mine[at:, :].astype(F32) + got[at:, :].astype(F32)).astype(total.dtype)


def line_kernel(*refs):
    parts, cold = refs[:-1], refs[-1]
    slices = cold.shape[1]
    sent = tree([part[0:slices, :].astype(F32) for part in parts]).astype(BF16)
    for peer in range(cold.shape[0]):
        cold[peer] = sent


def rows_kernel(maps, keys, hot_part, *refs):
    gathered, (pooled, slices_of, rows) = refs[:-3], refs[-3:]
    slices, width = maps.shape[2], pooled.shape[1]
    me = lax.axis_index("tt")
    looks = keys.shape[1]
    tiles = looks // LANES
    key = keys[0:1, :]
    halves = [jnp.zeros((width // 2, looks), F32) for _ in range(2)]
    for block, part in enumerate(gathered):
        for i in range(part.shape[0] // slices):
            pick = hot(iota((slices, looks), 0) + (me ^ (4 * i + block)) * slices == key)
            for side in range(2):
                turned = part[i * slices : (i + 1) * slices, side * slices : (side + 1) * slices]
                halves[side] = halves[side] + mm(turned, pick)
    total = jnp.concatenate(halves, axis=0)
    for t in range(tiles):
        slices_of[t] = total[:, t * LANES : (t + 1) * LANES]

    def forward(t, _):
        sums = [[jnp.zeros((E2, LANES), F32) for _ in range(E3)] for _ in range(E1)]
        for a in range(RANK):
            parts = [maps[t, e3 * RANK * E2 + a * E2 : e3 * RANK * E2 + a * E2 + E2, :] for e3 in range(E3)]
            for e1 in range(E1):
                entry = slices_of[t, e1 * RANK + a : e1 * RANK + a + 1, :]
                for e3 in range(E3):
                    sums[e1][e3] = sums[e1][e3] + parts[e3] * entry
        for e1 in range(E1):
            for e3 in range(E3):
                rows[t, pl.ds(e1 * TAIL + e3, E2, stride=E3), :] = sums[e1][e3]
        return 0

    lax.fori_loop(0, tiles, forward, 0)
    out = hot_part[...]
    for t in range(tiles):
        pick = hot(iota((pooled.shape[0], LANES), 0) == keys[1:2, t * LANES : (t + 1) * LANES])
        out = out + mm_nt(pick, rows[t].astype(BF16))
    pooled[...] = out


def final_kernel(first, mine, other, table, accum, *refs):
    parts, (new_first, new_table, new_accum) = refs[:-3], refs[-3:]
    total = tree([part[peer].astype(F32) for part in parts for peer in range(part.shape[0])])
    new_first[...] = first[...] - 0.01 * total
    lower = core_of() == 0
    grad = jnp.concatenate(
        [jnp.where(lower, mine[...], other[...]), jnp.where(lower, other[...], mine[...])], axis=0
    )
    rows = grad.shape[0]
    mean = jnp.mean(grad * grad, axis=1, keepdims=True)
    held = jnp.broadcast_to(accum[...], (LANES, rows)).T + mean
    new_accum[...] = held.T[0:1, :]
    new_table[...] = table[...] - 0.1 * grad / (jnp.sqrt(held[:, 0:1]) + 1e-08)


def local(
    hot_table, hot_accum, hot_owner, hot_row, hot_bag, cold_owner, first_index,
    mid_index, last_index, cold_bag, core_first, core_mid, core_last, bag_grads,
):
    rows, width = hot_table.shape
    bags = bag_grads.shape[0]
    slices = core_first.shape[0]
    hot_peers, tt_peers = lax.axis_size("hot"), lax.axis_size("tt")
    pairs = tt_peers // 2
    looks = cold_bag.shape[1]
    assert max(rows, bags, hot_peers) <= 256
    owner = hot_owner.reshape(1, -1)
    slice_owner = cold_owner.reshape(1, -1)
    held = slices * pairs
    few = hot_peers <= FEW
    tiles = looks // LANES

    assert 2 * slices == width and slices == LANES
    given = (core_mid, core_last, mid_index, last_index, cold_bag, slice_owner, first_index)
    hot_pack, first_pack, bag_grads, *given = call(
        pack_kernel,
        (((1 if few else hot_peers, rows + bags + PAD, width), BF16), ((slices, width), BF16))
        + tuple((x.shape, x.dtype) for x in (bag_grads,) + given),
        (hot_table, bag_grads, owner, hot_row, hot_bag, core_first) + given,
        far=6 + len(given),
    )
    core_mid, core_last, mid_index, last_index, cold_bag, slice_owner, first_index = given

    def spread(x):
        if few:
            out = [x]
            for bits in range(1, hot_peers):
                out.append(swap(x, "hot", bits))
            return out
        return [lax.all_to_all(x, "hot", 0, 0, tiled=True)]

    hot_all = spread(hot_pack)
    keep, send, maps, keys = call(
        maps_kernel,
        (((held, width), F32), ((held, width), BF16), ((tiles, E3 * RANK * E2, LANES), F32), ((8, looks), jnp.int32)),
        (core_mid, core_last, mid_index, last_index, cold_bag, slice_owner, first_index, bag_grads),
        (
            ((core_mid.shape[1] // RANK * PITCH, LANES), F32),
            ((RANK * E2, RANK * core_mid.shape[0]), BF16),
            ((RANK * core_mid.shape[0], looks), BF16),
            ((RANK * E3, looks), F32),
            ((width, looks), F32),
            ((width, looks), F32),
        ),
    )
    got = swap(send, "tt", 1)

    hot_keep, hot_send, hot_part = call(
        hot_kernel, (((rows // 2, width), F32), ((rows // 2, width), BF16), ((bags, width), F32)), hot_all
    )
    hot_got = swap(hot_send, "tt", 1)

    shards = [first_pack]
    for bits in range(2, pairs, 2):
        shards.append(swap(first_pack, "tt", 2 * bits))
    half = rows // 2
    shard_own, *pieces = call(
        functools.partial(pair_kernel, pairs),
        (((slices * len(shards), width), BF16),)
        + tuple(((slices + (half if bits == 1 else 0), width), BF16) for bits in range(pairs)),
        (keep, got, hot_keep, hot_got, *shards),
    )
    parts = [pieces[0]]
    for bits in range(1, pairs):
        parts.append(swap(pieces[bits], "tt", 2 * bits))
    neighbour = swap(shard_own, "tt", 2)

    mine, theirs, at, bits = pieces[1], parts[1], slices, 2
    while bits < pairs:
        (mine,) = call(functools.partial(step_kernel, at), (((half, width), BF16),), (mine, theirs))
        theirs = swap(mine, "tt", 2 * bits)
        at, bits = 0, 2 * bits
    (hot_half,) = call(functools.partial(step_kernel, at), (((half, width), F32),), (mine, theirs))
    hot_other = swap(hot_half, "tt", 1)
    own_other = swap(shard_own, "tt", 1)
    neighbour_other = swap(neighbour, "tt", 1)
    first_all = (shard_own, own_other, neighbour, neighbour_other)

    (cold_send,) = call(line_kernel, (((1 if few else hot_peers, slices, width), BF16),), parts)
    cold_all = spread(cold_send)

    (pooled,) = call(
        rows_kernel, (((bags, width), F32),),
        (maps, keys, hot_part, *first_all),
        (((tiles, width, LANES), F32), ((tiles, width, LANES), F32)),
    )

    new_first, new_table, new_accum = call(
        final_kernel,
        (((slices, width), F32), ((rows, width), F32), ((1, rows), F32)),
        (core_first, hot_half, hot_other, hot_table, hot_accum.reshape(1, -1), *cold_all),
    )
    return pooled, new_table, new_accum.reshape(-1), new_first


def solution(mesh):
    both = P(("hot", "tt"), None)
    placed = (
        P("hot", None), P("hot"), both, both, both, both, both, both, both, both,
        P("tt", None), P(), P(), both,
    )

    return jax.shard_map(
        local,
        mesh=mesh,
        in_specs=placed,
        out_specs=(both, P("hot", None), P("hot"), P("tt", None)),
        check_vma=False,
    )
```

```python
import functools
import math

import jax
import jax.numpy as jnp
from jax import lax
from jax.experimental import pallas as pl
from jax.experimental.pallas import tpu as pltpu
from jax.sharding import PartitionSpec as P


E1 = 8
E2 = 8
E3 = 4
RANK = 32
TAIL = E2 * E3
LANES = 128
PAD = 16
PITCH = RANK + 1
STEP = E2 + 1
FEW = 8
F32 = jnp.float32
BF16 = jnp.bfloat16
NT = (((1,), (1,)), ((), ()))


def iota(shape, dim):
    return lax.broadcasted_iota(jnp.int32, shape, dim)


def hot(mask):
    return mask.astype(F32).astype(BF16)


def mm(a, b):
    return jnp.dot(a, b, preferred_element_type=F32)


def mm_nt(a, b):
    return lax.dot_general(a, b, NT, preferred_element_type=F32)


def call(body, outs, args, scratch=(), far=0, spare=4 << 20):
    size = lambda shape, kind: math.prod(shape[:-2]) * max(shape[-2], 8) * max(shape[-1], LANES) * jnp.dtype(kind).itemsize
    scratch = tuple((x.shape, x.dtype) for x in args[:far]) + tuple(scratch)
    held = sum(size(a.shape, a.dtype) for a in args[far:]) + sum(size(*o) for o in tuple(outs) + scratch)
    near = len(args) - far

    def kernel(*refs):
        if not far:
            return body(*refs)
        given, rest, sem = refs[:far], refs[far:-1], refs[-1]
        taken = rest[near + len(outs) :]
        copies = [pltpu.make_async_copy(given[i], taken[i], sem.at[i]) for i in range(far)]
        for copy in copies:
            copy.start()
        for copy in copies:
            copy.wait()
        body(*taken[:far], *rest[: near + len(outs)], *taken[far:])

    args = [pltpu.with_memory_space_constraint(x, pltpu.HBM) for x in args[:far]] + list(args[far:])
    return pl.pallas_call(
        kernel,
        out_shape=tuple(jax.ShapeDtypeStruct(s, d) for s, d in outs),
        in_specs=[pl.BlockSpec(memory_space=pltpu.HBM)] * far + [pl.BlockSpec(memory_space=pltpu.VMEM)] * near,
        out_specs=(pl.BlockSpec(memory_space=pltpu.VMEM),) * len(outs),
        scratch_shapes=[pltpu.VMEM(s, d) for s, d in scratch]
        + ([pltpu.SemaphoreType.DMA((far,))] if far else []),
        compiler_params=pltpu.CompilerParams(vmem_limit_bytes=held + spare),
        cost_estimate=pl.CostEstimate(flops=2 * 10**9, bytes_accessed=10 << 20, transcendentals=0) if far else None,
    )(*args)


def core_of():
    return lax.axis_index("tt") & 1


def tree(parts):
    while len(parts) > 1:
        parts = [parts[i] + parts[i + 1] for i in range(0, len(parts), 2)]
    return parts[0]


def swap(x, axis, bits):
    return lax.ppermute(x, axis, [(i, i ^ bits) for i in range(lax.axis_size(axis))])


def pack_kernel(table, grads, owner, row, bag, first, *refs):
    count = len(refs) // 2 - 1
    hot_out, first_out = refs[count : count + 2]
    for src, dst in zip((grads,) + refs[:count], refs[count + 2 :]):
        dst[...] = src[...]
    rows, bags = table.shape[0], grads.shape[0]
    lower = first_out.shape[0]
    looks = jnp.concatenate(
        [owner[...], row[...], bag[...], jnp.zeros((PAD - 3, row.shape[1]), jnp.int32)], axis=0
    )
    turned = first[...].T.astype(BF16)
    for peer in range(hot_out.shape[0]):
        hot_out[peer, 0:rows, :] = table[...].astype(BF16)
        hot_out[peer, rows : rows + bags, :] = grads[...]
        hot_out[peer, rows + bags :, :] = looks.astype(F32).astype(BF16)
    first_out[...] = jnp.concatenate([turned[0:lower], turned[lower:]], axis=1)


def maps_kernel(
    mid, last, mid_index, last_index, bag, owner, index, grads,
    keep, send, maps, keys, turned, left, right, lasts_of, cot, terms,
):
    mids, lasts = mid.shape[0], last.shape[0]
    looks = bag.shape[1]

    blocks = mid.shape[1] // (2 * LANES)

    def turn(t, _):
        block = jnp.concatenate(
            [mid[:, pl.ds(pl.multiple_of((t + half) * LANES, LANES), LANES)] for half in (0, blocks)], axis=0
        ).astype(F32).T
        for part in range(LANES // RANK):
            turned[pl.ds((t * (LANES // RANK) + part) * PITCH, RANK), :] = block[part * RANK : (part + 1) * RANK, :]
        return 0

    lax.fori_loop(0, blocks, turn, 0, unroll=8)
    count = RANK * E2 // 2
    first_half = iota((count, 2 * mids), 1) < mids
    for pair in range(RANK // 2):
        low = turned[pl.ds(2 * pair, count, stride=PITCH), :]
        high = turned[pl.ds(2 * pair + 1, count, stride=PITCH), :]
        at = slice(pair * 2 * mids, (pair + 1) * 2 * mids)
        left[0:count, at] = jnp.where(first_half, low, pltpu.roll(high, mids, 1)).astype(BF16)
        left[count:, at] = jnp.where(first_half, pltpu.roll(low, mids, 1), high).astype(BF16)
    pick_last = hot(iota((lasts, looks), 0) == last_index[...])
    lasts_of[...] = mm(last[...].astype(F32).T.astype(BF16), pick_last)
    pick_bag = hot(iota((grads.shape[0], looks), 0) == bag[...])
    cot[...] = mm(grads[...].astype(F32).T.astype(BF16), pick_bag)
    pick_mid = hot(iota((mids, looks), 0) == mid_index[...])
    for e3 in range(E3):
        for b in range(RANK):
            at = b * E3 + e3
            spread = jnp.broadcast_to(lasts_of[at : at + 1, :], (PAD, looks)).astype(BF16)
            for part in range(0, mids, PAD):
                right[b * mids + part : b * mids + part + PAD, :] = pick_mid[part : part + PAD, :] * spread
        made = mm(left[...], right[...]).astype(BF16).astype(F32)
        for t in range(looks // LANES):
            for a in range(RANK):
                at = (e3 * RANK + a) * STEP
                maps[t, at : at + E2, :] = made[a * E2 : (a + 1) * E2, t * LANES : (t + 1) * LANES]

    def back(t, _):
        lanes = pl.ds(pl.multiple_of(t * LANES, LANES), LANES)
        for first in range(0, E1, E1 // 2):
            sums = [jnp.zeros((RANK, LANES), F32) for _ in range(E1 // 2)]
            for e2 in range(E2):
                for e3 in range(E3):
                    part = maps[t, pl.ds(e3 * RANK * STEP + e2, RANK, stride=STEP), :]
                    for i in range(E1 // 2):
                        at = (first + i) * TAIL + e2 * E3 + e3
                        sums[i] = sums[i] + part * cot[at : at + 1, lanes]
            for i in range(E1 // 2):
                terms[(first + i) * RANK : (first + i + 1) * RANK, lanes] = sums[i]
        return 0

    lax.fori_loop(0, looks // LANES, back, 0)
    whole = terms[...].astype(BF16)
    own = owner[...]
    held = keep.shape[0]
    slices = held // (lax.axis_size("tt") // 2)
    key = ((own & 1) ^ core_of()) * held + (own >> 1) * slices + index[...]
    step = min(held, 256)
    keys[0:1, :] = own * slices + index[...]
    keys[1:2, :] = bag[...]
    for half, out in ((0, keep), (1, send)):
        for start in range(0, held, step):
            pick = hot(iota((step, looks), 0) + (half * held + start) == key)
            out[start : start + step, :] = mm_nt(pick, whole).astype(out.dtype)


def packs_of(gathered):
    me = lax.axis_index("hot")
    if len(gathered) > 1:
        return [(me ^ bits, part.at[0]) for bits, part in enumerate(gathered)], gathered[0].at[0]
    whole = gathered[0]
    return [(peer, whole.at[peer]) for peer in range(whole.shape[0])], whole.at[me]


def lookups_of(part, at):
    sent = part[at:, :].astype(F32).astype(jnp.int32)
    return sent[0:1, :], sent[1:2, :], sent[2:3, :]


def hot_kernel(bags, *refs):
    gathered, (keep, send) = refs[:-2], refs[-2:]
    half = keep.shape[0]
    rows = 2 * half
    grad = jnp.zeros((rows, keep.shape[1]), F32)
    for peer, part in packs_of(gathered)[0]:
        owner, place, bag = lookups_of(part, rows + bags)
        upper = (place >= half).astype(jnp.int32)
        place = (upper ^ core_of()) * half + place - upper * half
        pick = hot((iota((rows, place.shape[1]), 0) == place) & (owner == lax.axis_index("hot")))
        count = mm_nt(pick, hot(iota((bags, bag.shape[1]), 0) == bag))
        grad = grad + mm(count.astype(BF16), part[rows : rows + bags, :])
    keep[...] = grad[0:half]
    send[...] = grad[half:].astype(BF16)


def bags_kernel(rows, *refs):
    gathered, pooled = refs[:-1], refs[-1]
    bags = pooled.shape[0]
    sources, mine = packs_of(gathered)
    owner, row, bag = lookups_of(mine, rows + bags)
    pick_bag = hot(iota((bags, bag.shape[1]), 0) == bag)
    total = jnp.zeros(pooled.shape, F32)
    for peer, part in sources:
        pick = hot((iota((rows, row.shape[1]), 0) == row) & (owner == peer))
        total = total + mm(mm_nt(pick_bag, pick).astype(BF16), part[0:rows, :])
    pooled[...] = total


def pair_kernel(pairs, cold_keep, cold_got, hot_keep, hot_got, *refs):
    shards, (held, own, *sends) = refs[:-1 - pairs], refs[-1 - pairs :]
    slices = own.shape[0]
    place = lax.axis_index("tt") >> 1
    for bits, out in enumerate((own, *sends)):
        at = pl.ds(pl.multiple_of((place ^ bits) * slices, slices), slices)
        out[0:slices, :] = (cold_keep[at, :] + cold_got[at, :].astype(F32)).astype(BF16)
    sends[0][slices:, :] = (hot_keep[...] + hot_got[...].astype(F32)).astype(BF16)
    for i, shard in enumerate(shards):
        held[i * slices : (i + 1) * slices, :] = shard[...]


def step_kernel(at, mine, got, total):
    total[...] = (mine[at:, :].astype(F32) + got[at:, :].astype(F32)).astype(total.dtype)


def line_kernel(*refs):
    parts, cold = refs[:-1], refs[-1]
    slices = cold.shape[1]
    sent = tree([part[0:slices, :].astype(F32) for part in parts]).astype(BF16)
    for peer in range(cold.shape[0]):
        cold[peer] = sent


def rows_kernel(maps, keys, hot_part, *refs):
    gathered, (pooled, slices_of, rows) = refs[:-3], refs[-3:]
    slices, width = maps.shape[2], pooled.shape[1]
    me = lax.axis_index("tt")
    looks = keys.shape[1]
    tiles = looks // LANES
    key = keys[0:1, :]
    halves = [jnp.zeros((width // 2, looks), F32) for _ in range(2)]
    for block, part in enumerate(gathered):
        for i in range(part.shape[0] // slices):
            pick = hot(iota((slices, looks), 0) + (me ^ (4 * i + block)) * slices == key)
            for side in range(2):
                turned = part[i * slices : (i + 1) * slices, side * slices : (side + 1) * slices]
                halves[side] = halves[side] + mm(turned, pick)
    total = jnp.concatenate(halves, axis=0)
    for t in range(tiles):
        slices_of[t] = total[:, t * LANES : (t + 1) * LANES]

    def forward(t, _):
        sums = [[jnp.zeros((E2, LANES), F32) for _ in range(E3)] for _ in range(E1)]
        for a in range(RANK):
            parts = [maps[t, (e3 * RANK + a) * STEP : (e3 * RANK + a) * STEP + E2, :] for e3 in range(E3)]
            for e1 in range(E1):
                entry = slices_of[t, e1 * RANK + a : e1 * RANK + a + 1, :]
                for e3 in range(E3):
                    sums[e1][e3] = sums[e1][e3] + parts[e3] * entry
        for e1 in range(E1):
            for e3 in range(E3):
                rows[t, pl.ds(e1 * TAIL + e3, E2, stride=E3), :] = sums[e1][e3]
        return 0

    lax.fori_loop(0, tiles, forward, 0)
    out = hot_part[...]
    for t in range(tiles):
        pick = hot(iota((pooled.shape[0], LANES), 0) == keys[1:2, t * LANES : (t + 1) * LANES])
        out = out + mm_nt(pick, rows[t].astype(BF16))
    pooled[...] = out


def final_kernel(first, mine, other, table, accum, *refs):
    parts, (new_first, new_table, new_accum) = refs[:-3], refs[-3:]
    total = tree([part[peer].astype(F32) for part in parts for peer in range(part.shape[0])])
    new_first[...] = first[...] - 0.01 * total
    lower = core_of() == 0
    grad = jnp.concatenate(
        [jnp.where(lower, mine[...], other[...]), jnp.where(lower, other[...], mine[...])], axis=0
    )
    rows = grad.shape[0]
    mean = jnp.mean(grad * grad, axis=1, keepdims=True)
    held = jnp.broadcast_to(accum[...], (LANES, rows)).T + mean
    new_accum[...] = held.T[0:1, :]
    new_table[...] = table[...] - 0.1 * grad / (jnp.sqrt(held[:, 0:1]) + 1e-08)


def local(
    hot_table, hot_accum, hot_owner, hot_row, hot_bag, cold_owner, first_index,
    mid_index, last_index, cold_bag, core_first, core_mid, core_last, bag_grads,
):
    rows, width = hot_table.shape
    bags = bag_grads.shape[0]
    slices = core_first.shape[0]
    hot_peers, tt_peers = lax.axis_size("hot"), lax.axis_size("tt")
    pairs = tt_peers // 2
    looks = cold_bag.shape[1]
    assert max(rows, bags, hot_peers) <= 256
    owner = hot_owner.reshape(1, -1)
    slice_owner = cold_owner.reshape(1, -1)
    held = slices * pairs
    few = hot_peers <= FEW
    tiles = looks // LANES

    assert 2 * slices == width and slices == LANES
    given = (core_last, mid_index, last_index, cold_bag, slice_owner, first_index)
    hot_pack, first_pack, bag_grads, *given = call(
        pack_kernel,
        (((1 if few else hot_peers, rows + bags + PAD, width), BF16), ((slices, width), BF16))
        + tuple((x.shape, x.dtype) for x in (bag_grads,) + given),
        (hot_table, bag_grads, owner, hot_row, hot_bag, core_first) + given,
        far=6 + len(given),
    )
    core_last, mid_index, last_index, cold_bag, slice_owner, first_index = given

    def spread(x):
        if few:
            out = [x]
            for bits in range(1, hot_peers):
                out.append(swap(x, "hot", bits))
            return out
        return [lax.all_to_all(x, "hot", 0, 0, tiled=True)]

    hot_all = spread(hot_pack)
    keep, send, maps, keys = call(
        maps_kernel,
        (((held, width), F32), ((held, width), BF16), ((tiles, E3 * RANK * STEP, LANES), F32), ((8, looks), jnp.int32)),
        (core_mid, core_last, mid_index, last_index, cold_bag, slice_owner, first_index, bag_grads),
        (
            ((RANK * E2 // 2 * PITCH, LANES), F32),
            ((RANK * E2, RANK * core_mid.shape[0]), BF16),
            ((RANK * core_mid.shape[0], looks), BF16),
            ((RANK * E3, looks), F32),
            ((width, looks), F32),
            ((width, looks), F32),
        ),
    )
    got = swap(send, "tt", 1)

    hot_keep, hot_send = call(
        functools.partial(hot_kernel, bags),
        (((rows // 2, width), F32), ((rows // 2, width), BF16)), hot_all,
    )
    (hot_part,) = call(functools.partial(bags_kernel, rows), (((bags, width), F32),), hot_all)
    hot_got = swap(hot_send, "tt", 1)

    shards = [first_pack]
    for bits in range(2, pairs, 2):
        shards.append(swap(first_pack, "tt", 2 * bits))
    half = rows // 2
    shard_own, *pieces = call(
        functools.partial(pair_kernel, pairs),
        (((slices * len(shards), width), BF16),)
        + tuple(((slices + (half if bits == 1 else 0), width), BF16) for bits in range(pairs)),
        (keep, got, hot_keep, hot_got, *shards),
    )
    parts = [pieces[0]]
    for bits in range(1, pairs):
        parts.append(swap(pieces[bits], "tt", 2 * bits))
    neighbour = swap(shard_own, "tt", 2)

    mine, theirs, at, bits = pieces[1], parts[1], slices, 2
    while bits < pairs:
        (mine,) = call(functools.partial(step_kernel, at), (((half, width), BF16),), (mine, theirs))
        theirs = swap(mine, "tt", 2 * bits)
        at, bits = 0, 2 * bits
    (hot_half,) = call(functools.partial(step_kernel, at), (((half, width), F32),), (mine, theirs))
    hot_other = swap(hot_half, "tt", 1)
    own_other = swap(shard_own, "tt", 1)
    neighbour_other = swap(neighbour, "tt", 1)
    first_all = (shard_own, own_other, neighbour, neighbour_other)

    (cold_send,) = call(line_kernel, (((1 if few else hot_peers, slices, width), BF16),), parts)
    cold_all = spread(cold_send)

    (pooled,) = call(
        rows_kernel, (((bags, width), F32),),
        (maps, keys, hot_part, *first_all),
        (((tiles, width, LANES), F32), ((tiles, width, LANES), F32)),
    )

    new_first, new_table, new_accum = call(
        final_kernel,
        (((slices, width), F32), ((rows, width), F32), ((1, rows), F32)),
        (core_first, hot_half, hot_other, hot_table, hot_accum.reshape(1, -1), *cold_all),
    )
    return pooled, new_table, new_accum.reshape(-1), new_first


def solution(mesh):
    both = P(("hot", "tt"), None)
    placed = (
        P("hot", None), P("hot"), both, both, both, both, both, both, both, both,
        P("tt", None), P(), P(), both,
    )

    return jax.shard_map(
        local,
        mesh=mesh,
        in_specs=placed,
        out_specs=(both, P("hot", None), P("hot"), P("tt", None)),
        check_vma=False,
    )
```

```python
import functools
import math

import jax
import jax.numpy as jnp
from jax import lax
from jax.experimental import pallas as pl
from jax.experimental.pallas import tpu as pltpu
from jax.sharding import PartitionSpec as P


E1 = 8
E2 = 8
E3 = 4
RANK = 32
TAIL = E2 * E3
LANES = 128
PAD = 16
PITCH = RANK + 1
STEP = E2 + 1
FEW = 8
F32 = jnp.float32
BF16 = jnp.bfloat16
NT = (((1,), (1,)), ((), ()))


def iota(shape, dim):
    return lax.broadcasted_iota(jnp.int32, shape, dim)


def hot(mask):
    return mask.astype(F32).astype(BF16)


def mm(a, b):
    return jnp.dot(a, b, preferred_element_type=F32)


def mm_nt(a, b):
    return lax.dot_general(a, b, NT, preferred_element_type=F32)


def call(body, outs, args, scratch=(), far=0, spare=4 << 20):
    size = lambda shape, kind: math.prod(shape[:-2]) * max(shape[-2], 8) * max(shape[-1], LANES) * jnp.dtype(kind).itemsize
    scratch = tuple((x.shape, x.dtype) for x in args[:far]) + tuple(scratch)
    held = sum(size(a.shape, a.dtype) for a in args[far:]) + sum(size(*o) for o in tuple(outs) + scratch)
    near = len(args) - far

    def kernel(*refs):
        if not far:
            return body(*refs)
        given, rest, sem = refs[:far], refs[far:-1], refs[-1]
        taken = rest[near + len(outs) :]
        copies = [pltpu.make_async_copy(given[i], taken[i], sem.at[i]) for i in range(far)]
        for copy in copies:
            copy.start()
        for copy in copies:
            copy.wait()
        body(*taken[:far], *rest[: near + len(outs)], *taken[far:])

    args = [pltpu.with_memory_space_constraint(x, pltpu.HBM) for x in args[:far]] + list(args[far:])
    return pl.pallas_call(
        kernel,
        out_shape=tuple(jax.ShapeDtypeStruct(s, d) for s, d in outs),
        in_specs=[pl.BlockSpec(memory_space=pltpu.HBM)] * far + [pl.BlockSpec(memory_space=pltpu.VMEM)] * near,
        out_specs=(pl.BlockSpec(memory_space=pltpu.VMEM),) * len(outs),
        scratch_shapes=[pltpu.VMEM(s, d) for s, d in scratch]
        + ([pltpu.SemaphoreType.DMA((far,))] if far else []),
        compiler_params=pltpu.CompilerParams(vmem_limit_bytes=held + spare),
        cost_estimate=pl.CostEstimate(flops=2 * 10**9, bytes_accessed=10 << 20, transcendentals=0) if far else None,
    )(*args)


def core_of():
    return lax.axis_index("tt") & 1


def tree(parts):
    while len(parts) > 1:
        parts = [parts[i] + parts[i + 1] for i in range(0, len(parts), 2)]
    return parts[0]


def swap(x, axis, bits):
    return lax.ppermute(x, axis, [(i, i ^ bits) for i in range(lax.axis_size(axis))])


def pack_kernel(table, grads, owner, row, bag, first, *refs):
    count = len(refs) // 2 - 1
    hot_out, first_out = refs[count : count + 2]
    for src, dst in zip((grads,) + refs[:count], refs[count + 2 :]):
        dst[...] = src[...]
    rows, bags = table.shape[0], grads.shape[0]
    lower = first_out.shape[0]
    looks = jnp.concatenate(
        [owner[...], row[...], bag[...], jnp.zeros((PAD - 3, row.shape[1]), jnp.int32)], axis=0
    )
    turned = first[...].T.astype(BF16)
    for peer in range(hot_out.shape[0]):
        hot_out[peer, 0:rows, :] = table[...].astype(BF16)
        hot_out[peer, rows : rows + bags, :] = grads[...]
        hot_out[peer, rows + bags :, :] = looks.astype(F32).astype(BF16)
    first_out[...] = jnp.concatenate([turned[0:lower], turned[lower:]], axis=1)


def maps_kernel(
    mid, last, mid_index, last_index, bag, owner, index, grads,
    keep, send, maps, keys, turned, left, right, lasts_of, cot, terms,
):
    mids, lasts = mid.shape[0], last.shape[0]
    looks = bag.shape[1]

    blocks = mid.shape[1] // (2 * LANES)

    def turn(t, _):
        block = jnp.concatenate(
            [mid[:, pl.ds(pl.multiple_of((t + half) * LANES, LANES), LANES)] for half in (0, blocks)], axis=0
        ).astype(F32).T
        for part in range(LANES // RANK):
            turned[pl.ds((t * (LANES // RANK) + part) * PITCH, RANK), :] = block[part * RANK : (part + 1) * RANK, :]
        return 0

    lax.fori_loop(0, blocks, turn, 0, unroll=8)
    count = RANK * E2 // 2
    first_half = iota((count, 2 * mids), 1) < mids
    for pair in range(RANK // 2):
        low = turned[pl.ds(2 * pair, count, stride=PITCH), :]
        high = turned[pl.ds(2 * pair + 1, count, stride=PITCH), :]
        at = slice(pair * 2 * mids, (pair + 1) * 2 * mids)
        left[0:count, at] = jnp.where(first_half, low, pltpu.roll(high, mids, 1)).astype(BF16)
        left[count:, at] = jnp.where(first_half, pltpu.roll(low, mids, 1), high).astype(BF16)
    pick_last = hot(iota((lasts, looks), 0) == last_index[...])
    lasts_of[...] = mm(last[...].astype(F32).T.astype(BF16), pick_last)
    pick_bag = hot(iota((grads.shape[0], looks), 0) == bag[...])
    cot[...] = mm(grads[...].astype(F32).T.astype(BF16), pick_bag)
    pick_mid = hot(iota((mids, looks), 0) == mid_index[...])
    for e3 in range(E3):
        for b in range(RANK):
            at = b * E3 + e3
            spread = jnp.broadcast_to(lasts_of[at : at + 1, :], (PAD, looks)).astype(BF16)
            for part in range(0, mids, PAD):
                right[b * mids + part : b * mids + part + PAD, :] = pick_mid[part : part + PAD, :] * spread
        made = mm(left[...], right[...]).astype(BF16).astype(F32)
        for t in range(looks // LANES):
            for a in range(RANK):
                at = (e3 * RANK + a) * STEP
                maps[t, at : at + E2, :] = made[a * E2 : (a + 1) * E2, t * LANES : (t + 1) * LANES]

    def back(t, _):
        lanes = pl.ds(pl.multiple_of(t * LANES, LANES), LANES)
        for first in range(0, E1, E1 // 2):
            sums = [jnp.zeros((RANK, LANES), F32) for _ in range(E1 // 2)]
            for e2 in range(E2):
                for e3 in range(E3):
                    part = maps[t, pl.ds(e3 * RANK * STEP + e2, RANK, stride=STEP), :]
                    for i in range(E1 // 2):
                        at = (first + i) * TAIL + e2 * E3 + e3
                        sums[i] = sums[i] + part * cot[at : at + 1, lanes]
            for i in range(E1 // 2):
                terms[(first + i) * RANK : (first + i + 1) * RANK, lanes] = sums[i]
        return 0

    lax.fori_loop(0, looks // LANES, back, 0)
    whole = terms[...].astype(BF16)
    own = owner[...]
    held = keep.shape[0]
    slices = held // (lax.axis_size("tt") // 2)
    key = ((own & 1) ^ core_of()) * held + (own >> 1) * slices + index[...]
    step = min(held, 256)
    keys[0:1, :] = own * slices + index[...]
    keys[1:2, :] = bag[...]
    for half, out in ((0, keep), (1, send)):
        for start in range(0, held, step):
            pick = hot(iota((step, looks), 0) + (half * held + start) == key)
            out[start : start + step, :] = mm_nt(pick, whole).astype(out.dtype)


def packs_of(gathered):
    me = lax.axis_index("hot")
    if len(gathered) > 1:
        return [(me ^ bits, part.at[0]) for bits, part in enumerate(gathered)], gathered[0].at[0]
    whole = gathered[0]
    return [(peer, whole.at[peer]) for peer in range(whole.shape[0])], whole.at[me]


def lookups_of(part, at):
    sent = part[at:, :].astype(F32).astype(jnp.int32)
    return sent[0:1, :], sent[1:2, :], sent[2:3, :]


def hot_kernel(bags, *refs):
    gathered, (keep, send) = refs[:-2], refs[-2:]
    half = keep.shape[0]
    rows = 2 * half
    grad = jnp.zeros((rows, keep.shape[1]), F32)
    for peer, part in packs_of(gathered)[0]:
        owner, place, bag = lookups_of(part, rows + bags)
        upper = (place >= half).astype(jnp.int32)
        place = (upper ^ core_of()) * half + place - upper * half
        pick = hot((iota((rows, place.shape[1]), 0) == place) & (owner == lax.axis_index("hot")))
        count = mm_nt(pick, hot(iota((bags, bag.shape[1]), 0) == bag))
        grad = grad + mm(count.astype(BF16), part[rows : rows + bags, :])
    keep[...] = grad[0:half]
    send[...] = grad[half:].astype(BF16)


def bags_kernel(rows, keys, own, other, *refs):
    gathered, (pooled, near) = refs[:-2], refs[-2:]
    near[...] = slices_from(keys, ((0, own), (1, other)), near.shape[0])
    bags = pooled.shape[0]
    sources, mine = packs_of(gathered)
    owner, row, bag = lookups_of(mine, rows + bags)
    pick_bag = hot(iota((bags, bag.shape[1]), 0) == bag)
    total = jnp.zeros(pooled.shape, F32)
    for peer, part in sources:
        pick = hot((iota((rows, row.shape[1]), 0) == row) & (owner == peer))
        total = total + mm(mm_nt(pick_bag, pick).astype(BF16), part[0:rows, :])
    pooled[...] = total


def pair_kernel(pairs, cold_keep, cold_got, hot_keep, hot_got, *refs):
    shards, (held, own, *sends) = refs[:-1 - pairs], refs[-1 - pairs :]
    slices = own.shape[0]
    place = lax.axis_index("tt") >> 1
    for bits, out in enumerate((own, *sends)):
        at = pl.ds(pl.multiple_of((place ^ bits) * slices, slices), slices)
        out[0:slices, :] = (cold_keep[at, :] + cold_got[at, :].astype(F32)).astype(BF16)
    sends[0][slices:, :] = (hot_keep[...] + hot_got[...].astype(F32)).astype(BF16)
    for i, shard in enumerate(shards):
        held[i * slices : (i + 1) * slices, :] = shard[...]


def step_kernel(at, mine, got, total):
    total[...] = (mine[at:, :].astype(F32) + got[at:, :].astype(F32)).astype(total.dtype)


def line_kernel(*refs):
    parts, cold = refs[:-1], refs[-1]
    slices = cold.shape[1]
    sent = tree([part[0:slices, :].astype(F32) for part in parts]).astype(BF16)
    for peer in range(cold.shape[0]):
        cold[peer] = sent


def slices_from(keys, blocks, width):
    slices, looks = LANES, keys.shape[1]
    me = lax.axis_index("tt")
    halves = [jnp.zeros((width // 2, looks), F32) for _ in range(2)]
    for block, part in blocks:
        for i in range(part.shape[0] // slices):
            pick = hot(iota((slices, looks), 0) + (me ^ (4 * i + block)) * slices == keys[0:1, :])
            for side in range(2):
                turned = part[i * slices : (i + 1) * slices, side * slices : (side + 1) * slices]
                halves[side] = halves[side] + mm(turned, pick)
    return jnp.concatenate(halves, axis=0)


def rows_kernel(maps, keys, hot_part, near, third, fourth, pooled, slices_of, rows):
    width, looks = near.shape
    tiles = looks // LANES
    total = near[...] + slices_from(keys, ((2, third), (3, fourth)), width)
    for t in range(tiles):
        slices_of[t] = total[:, t * LANES : (t + 1) * LANES]

    def forward(t, _):
        sums = [[jnp.zeros((E2, LANES), F32) for _ in range(E3)] for _ in range(E1)]
        for a in range(RANK):
            parts = [maps[t, (e3 * RANK + a) * STEP : (e3 * RANK + a) * STEP + E2, :] for e3 in range(E3)]
            for e1 in range(E1):
                entry = slices_of[t, e1 * RANK + a : e1 * RANK + a + 1, :]
                for e3 in range(E3):
                    sums[e1][e3] = sums[e1][e3] + parts[e3] * entry
        for e1 in range(E1):
            for e3 in range(E3):
                rows[t, pl.ds(e1 * TAIL + e3, E2, stride=E3), :] = sums[e1][e3]
        return 0

    lax.fori_loop(0, tiles, forward, 0)
    out = hot_part[...]
    for t in range(tiles):
        pick = hot(iota((pooled.shape[0], LANES), 0) == keys[1:2, t * LANES : (t + 1) * LANES])
        out = out + mm_nt(pick, rows[t].astype(BF16))
    pooled[...] = out


def final_kernel(first, mine, other, table, accum, *refs):
    parts, (new_first, new_table, new_accum) = refs[:-3], refs[-3:]
    total = tree([part[peer].astype(F32) for part in parts for peer in range(part.shape[0])])
    new_first[...] = first[...] - 0.01 * total
    lower = core_of() == 0
    grad = jnp.concatenate(
        [jnp.where(lower, mine[...], other[...]), jnp.where(lower, other[...], mine[...])], axis=0
    )
    rows = grad.shape[0]
    mean = jnp.mean(grad * grad, axis=1, keepdims=True)
    held = jnp.broadcast_to(accum[...], (LANES, rows)).T + mean
    new_accum[...] = held.T[0:1, :]
    new_table[...] = table[...] - 0.1 * grad / (jnp.sqrt(held[:, 0:1]) + 1e-08)


def local(
    hot_table, hot_accum, hot_owner, hot_row, hot_bag, cold_owner, first_index,
    mid_index, last_index, cold_bag, core_first, core_mid, core_last, bag_grads,
):
    rows, width = hot_table.shape
    bags = bag_grads.shape[0]
    slices = core_first.shape[0]
    hot_peers, tt_peers = lax.axis_size("hot"), lax.axis_size("tt")
    pairs = tt_peers // 2
    looks = cold_bag.shape[1]
    assert max(rows, bags, hot_peers) <= 256
    owner = hot_owner.reshape(1, -1)
    slice_owner = cold_owner.reshape(1, -1)
    held = slices * pairs
    few = hot_peers <= FEW
    tiles = looks // LANES

    assert 2 * slices == width and slices == LANES
    given = (core_last, mid_index, last_index, cold_bag, slice_owner, first_index)
    hot_pack, first_pack, bag_grads, *given = call(
        pack_kernel,
        (((1 if few else hot_peers, rows + bags + PAD, width), BF16), ((slices, width), BF16))
        + tuple((x.shape, x.dtype) for x in (bag_grads,) + given),
        (hot_table, bag_grads, owner, hot_row, hot_bag, core_first) + given,
        far=6 + len(given),
    )
    core_last, mid_index, last_index, cold_bag, slice_owner, first_index = given

    def spread(x):
        if few:
            out = [x]
            for bits in range(1, hot_peers):
                out.append(swap(x, "hot", bits))
            return out
        return [lax.all_to_all(x, "hot", 0, 0, tiled=True)]

    hot_all = spread(hot_pack)
    keep, send, maps, keys = call(
        maps_kernel,
        (((held, width), F32), ((held, width), BF16), ((tiles, E3 * RANK * STEP, LANES), F32), ((8, looks), jnp.int32)),
        (core_mid, core_last, mid_index, last_index, cold_bag, slice_owner, first_index, bag_grads),
        (
            ((RANK * E2 // 2 * PITCH, LANES), F32),
            ((RANK * E2, RANK * core_mid.shape[0]), BF16),
            ((RANK * core_mid.shape[0], looks), BF16),
            ((RANK * E3, looks), F32),
            ((width, looks), F32),
            ((width, looks), F32),
        ),
    )
    got = swap(send, "tt", 1)

    hot_keep, hot_send = call(
        functools.partial(hot_kernel, bags),
        (((rows // 2, width), F32), ((rows // 2, width), BF16)), hot_all,
    )
    hot_got = swap(hot_send, "tt", 1)

    shards = [first_pack]
    for bits in range(2, pairs, 2):
        shards.append(swap(first_pack, "tt", 2 * bits))
    half = rows // 2
    shard_own, *pieces = call(
        functools.partial(pair_kernel, pairs),
        (((slices * len(shards), width), BF16),)
        + tuple(((slices + (half if bits == 1 else 0), width), BF16) for bits in range(pairs)),
        (keep, got, hot_keep, hot_got, *shards),
    )
    parts = [pieces[0]]
    for bits in range(1, pairs):
        parts.append(swap(pieces[bits], "tt", 2 * bits))
    neighbour = swap(shard_own, "tt", 2)

    mine, theirs, at, bits = pieces[1], parts[1], slices, 2
    while bits < pairs:
        (mine,) = call(functools.partial(step_kernel, at), (((half, width), BF16),), (mine, theirs))
        theirs = swap(mine, "tt", 2 * bits)
        at, bits = 0, 2 * bits
    (hot_half,) = call(functools.partial(step_kernel, at), (((half, width), F32),), (mine, theirs))
    hot_other = swap(hot_half, "tt", 1)
    own_other = swap(shard_own, "tt", 1)
    hot_part, near = call(
        functools.partial(bags_kernel, rows), (((bags, width), F32), ((width, looks), F32)),
        (keys, shard_own, own_other, *hot_all),
    )
    neighbour_other = swap(neighbour, "tt", 1)

    (cold_send,) = call(line_kernel, (((1 if few else hot_peers, slices, width), BF16),), parts)
    cold_all = spread(cold_send)

    (pooled,) = call(
        rows_kernel, (((bags, width), F32),),
        (maps, keys, hot_part, near, neighbour, neighbour_other),
        (((tiles, width, LANES), F32), ((tiles, width, LANES), F32)),
    )

    new_first, new_table, new_accum = call(
        final_kernel,
        (((slices, width), F32), ((rows, width), F32), ((1, rows), F32)),
        (core_first, hot_half, hot_other, hot_table, hot_accum.reshape(1, -1), *cold_all),
    )
    return pooled, new_table, new_accum.reshape(-1), new_first


def solution(mesh):
    both = P(("hot", "tt"), None)
    placed = (
        P("hot", None), P("hot"), both, both, both, both, both, both, both, both,
        P("tt", None), P(), P(), both,
    )

    return jax.shard_map(
        local,
        mesh=mesh,
        in_specs=placed,
        out_specs=(both, P("hot", None), P("hot"), P("tt", None)),
        check_vma=False,
    )
```
